32 devices in a mesh: band: 4 (over y, x), dx: 2 (over core), dy: 4 (over z).
Axes of the slice: x: 2, y: 2, z: 4, core: 2. Of those that a mesh axis runs over, the one named last changes fastest.
Arguments:
- psi: bfloat16 [256, 4, 32, 128], P('band', 'dx', 'dy')
- base_potential: float32 [4, 32, 128], P('dx', 'dy'), may hold values from -1 to 1
- defect_site: int32 [4, 32, 128], P('dx', 'dy'), may hold values from 0 to 7
- defect_level: float32 [8], replicated, may hold values from -2 to 2
Outputs:
- filtered: bfloat16 [256, 4, 32, 128], P('band', 'dx', 'dy')
- correlation: float32 [256, 256], P('band', 'dy')
The draws below stay inside these ranges and needn't reach their ends.
All inputs are finite; a program needn't handle non-finite values.
Results may differ from the reference program's by a relative error of at most 0.006.
Values may be sent and summed in bfloat16 or wider, within the bound.
A program may use at most 64 MiB of HBM per device.

```python
import jax
import jax.numpy as jnp
from jax import lax

NB_DEV = 64
NZ = 128
DEFECTS = 8
NB = 256
NX = 4
NY = 32
N_BAND = 4


def draw_psi(key, part):
    keys = jax.random.split(key, 3)
    noise = jax.random.normal(keys[0], (NB, NX, NY, NZ), jnp.float32)
    common = jax.random.normal(keys[1], (2, 1, NX, NY, NZ), jnp.float32)
    weights = jax.random.uniform(keys[2], (2, NB, 1, 1, 1), jnp.float32, -0.8, 0.8)
    field = noise + weights[0] * common[0] + weights[1] * common[1]
    xpos = jnp.arange(NX, dtype=jnp.float32) / NX
    ypos = jnp.arange(NY, dtype=jnp.float32) / NY
    envelope = (1.0 + 0.35 * xpos)[:, None, None] * (1.0 + 0.35 * ypos)[None, :, None]
    return (field * envelope[None]).astype(jnp.bfloat16)


def with_ends(array, rng, smallest, largest):
    index_at = [jax.random.randint(jax.random.fold_in(rng, axis), (), 0, length) for axis, length in enumerate(array.shape)]
    main_axis = array.shape.index(max(array.shape))
    beside = index_at[:main_axis] + [(index_at[main_axis] + 1) % array.shape[main_axis]] + index_at[main_axis + 1:]
    return array.at[tuple(index_at)].set(smallest).at[tuple(beside)].set(largest)


def steps_of(own_key, shape, shards, smallest, top_value):
    level, own = 1.0, jax.random.fold_in(own_key, 6)
    for position, blocks in shards:
        steps = jnp.exp(jax.random.uniform(jax.random.fold_in(own, position), (blocks,), jnp.float32, smallest / len(shards), top_value / len(shards)))
        level = level * jnp.repeat(steps, shape[position] // blocks).reshape([-1 if axis == position else 1 for axis in range(len(shape))])
    return level


def setup_inputs(seed: int = 0) -> dict:
    splits = jax.random.split(jax.random.key(seed), 5)
    return {
        "psi": draw_psi(jax.random.fold_in(splits[4], 71), 0),
        "base_potential": jnp.clip(jax.random.uniform(splits[1], (NX, NY, NZ), jnp.float32, -1.0, 1.0) * steps_of(splits[1], (NX, NY, NZ), ((0, 2), (1, 4)), -0.4, 0.0), -1.0, 1.0),
        "defect_site": with_ends(jax.random.randint(splits[2], (NX, NY, NZ), 0, DEFECTS), jax.random.fold_in(splits[2], 1), 0, DEFECTS - 1).astype(jnp.int32),
        "defect_level": jnp.clip(jax.random.uniform(splits[3], (DEFECTS,), jnp.float32, -2.0, 2.0), -2.0, 2.0),
    }


SELF_WEIGHT = -2.5
NEAR_WEIGHT = 4.0 / 3.0
FAR_WEIGHT = -1.0 / 12.0
FILTER_CENTER = 5.5
FILTER_HALF = 3.5


def potential_of(base_potential, defect_site, defect_level):
    levels = jnp.arange(defect_level.shape[0], dtype=jnp.int32)
    picked = jnp.sum(jnp.where(defect_site[None] == levels[:, None, None, None], defect_level[:, None, None, None], jnp.float32(0.0)), axis=0)
    return base_potential + picked


def hamiltonian(field, potential):
    laplace = 3.0 * SELF_WEIGHT * field
    for axis_number in (1, 2, 3):
        laplace = laplace + NEAR_WEIGHT * (jnp.roll(field, 1, axis_number) + jnp.roll(field, -1, axis_number))
        laplace = laplace + FAR_WEIGHT * (jnp.roll(field, 2, axis_number) + jnp.roll(field, -2, axis_number))
    return -0.5 * laplace + potential[None] * field


def filter_block(block, potential):
    start_field = block.astype(jnp.float32)
    first = ((hamiltonian(start_field, potential) - FILTER_CENTER * start_field) / FILTER_HALF).astype(jnp.bfloat16)
    first_wide = first.astype(jnp.float32)
    second = 2.0 * (hamiltonian(first_wide, potential) - FILTER_CENTER * first_wide) / FILTER_HALF - start_field
    return second.astype(jnp.bfloat16)


def reference(psi, base_potential, defect_site, defect_level):
    potential = potential_of(base_potential, defect_site, defect_level)
    blocks = psi.reshape(N_BAND, NB_DEV, NX, NY, NZ)
    filtered = lax.map(lambda single: filter_block(single, potential), blocks).reshape(NB, NX, NY, NZ)
    flat = filtered.reshape(NB, NX * NY * NZ)
    correlation = jnp.dot(flat, flat.T, preferred_element_type=jnp.float32) / (NX * NY * NZ)
    return filtered, correlation
```

```python
import functools

import jax
import jax.numpy as jnp
from jax import lax
from jax.experimental import pallas as pl
from jax.experimental.pallas import tpu as pltpu
from jax.sharding import PartitionSpec as P

SELF_WEIGHT = -2.5
NEAR_WEIGHT = 4.0 / 3.0
FAR_WEIGHT = -1.0 / 12.0
FILTER_CENTER = 5.5
FILTER_HALF = 3.5


def with_halo(block, sides, width):
    for axis, dim in sides:
        count = lax.axis_size(axis)
        forward = [(i, i + 1) for i in range(count - 1)]
        forward.append((count - 1, 0))
        backward = [(target, source) for source, target in forward]
        low = lax.ppermute(
            lax.slice_in_dim(block, block.shape[dim] - width, None, axis=dim), axis, forward
        )
        high = lax.ppermute(lax.slice_in_dim(block, 0, width, axis=dim), axis, backward)
        block = jnp.concatenate([low, block, high], axis=dim)
    return block


def hamiltonian(field, potential):
    padded = with_halo(field, (("dx", 1), ("dy", 2)), 2).astype(jnp.float32)
    width_x = field.shape[1]
    width_y = field.shape[2]
    center = padded[:, 2 : 2 + width_x, 2 : 2 + width_y, :]
    laplace = 3.0 * SELF_WEIGHT * center
    laplace = laplace + NEAR_WEIGHT * (
        padded[:, 3 : 3 + width_x, 2 : 2 + width_y, :]
        + padded[:, 1 : 1 + width_x, 2 : 2 + width_y, :]
    )
    laplace = laplace + FAR_WEIGHT * (
        padded[:, 4 : 4 + width_x, 2 : 2 + width_y, :] + padded[:, 0:width_x, 2 : 2 + width_y, :]
    )
    laplace = laplace + NEAR_WEIGHT * (
        padded[:, 2 : 2 + width_x, 3 : 3 + width_y, :]
        + padded[:, 2 : 2 + width_x, 1 : 1 + width_y, :]
    )
    laplace = laplace + FAR_WEIGHT * (
        padded[:, 2 : 2 + width_x, 4 : 4 + width_y, :] + padded[:, 2 : 2 + width_x, 0:width_y, :]
    )
    laplace = laplace + NEAR_WEIGHT * (jnp.roll(center, 1, 3) + jnp.roll(center, -1, 3))
    laplace = laplace + FAR_WEIGHT * (jnp.roll(center, 2, 3) + jnp.roll(center, -2, 3))
    return (-0.5 * laplace + potential[None] * center, center)


def shards(psi, base_potential, defect_site, defect_level):
    levels = jnp.arange(defect_level.shape[0], dtype=jnp.int32)
    picked = jnp.sum(
        jnp.where(
            defect_site[None] == levels[:, None, None, None],
            defect_level[:, None, None, None],
            jnp.float32(0.0),
        ),
        axis=0,
    )
    potential = base_potential + picked
    applied, start_field = hamiltonian(psi, potential)
    first = ((applied - FILTER_CENTER * start_field) / FILTER_HALF).astype(jnp.bfloat16)
    applied_next, first_wide = hamiltonian(first, potential)
    filtered = (
        2.0 * (applied_next - FILTER_CENTER * first_wide) / FILTER_HALF - start_field
    ).astype(jnp.bfloat16)
    nb_dev = psi.shape[0]
    cells_all = (
        psi.shape[1] * psi.shape[2] * psi.shape[3] * lax.axis_size("dx") * lax.axis_size("dy")
    )
    flat = filtered.reshape(nb_dev, -1)
    tile = lax.dot_general(
        flat,
        lax.all_gather(flat, "band", axis=0, tiled=True),
        (((1,), (1,)), ((), ())),
        preferred_element_type=jnp.float32,
    )
    column_part = lax.psum_scatter(
        tile.astype(jnp.bfloat16), "dy", scatter_dimension=1, tiled=True
    ).astype(jnp.float32)
    columns = lax.psum(column_part, "dx")
    correlation = columns / cells_all
    return (filtered, correlation)


MESH = pl.DeviceIdType.MESH
CHUNKS = 2


def apply_filter(load, x, j, coef):
    center = load(x, j)
    near = load((x + 1) % 4, j) + load((x + 3) % 4, j)
    far_x = load((x + 2) % 4, j)
    far = far_x + far_x
    near = near + load(x, j + 1) + load(x, j - 1)
    far = far + load(x, j + 2) + load(x, j - 2)
    near = near + pltpu.roll(center, 1, 1) + pltpu.roll(center, 127, 1)
    far = far + pltpu.roll(center, 2, 1) + pltpu.roll(center, 126, 1)
    rows = center.shape[0]
    scaled = (center.reshape(rows // 8, 8, 128) * coef[None]).reshape(rows, 128)
    return (
        scaled
        + near * (-0.5 * NEAR_WEIGHT / FILTER_HALF)
        + far * (-0.5 * FAR_WEIGHT / FILTER_HALF)
    )


def over(low, high, body, part):
    group = next(size for size in (8, 4, 2, 1) if (high - low) % size == 0)

    def step(i, carry):
        for k in range(group):
            body(part, low + i * group + k)
        return carry

    lax.fori_loop(0, (high - low) // group, step, 0)


def kernel(
    n_band, n_dy, cells_all,
    level_hbm, psi_hbm, base_hbm, site_hbm,
    out_ref, corr_ref,
    level_ref, psi_ref, base_ref, site_ref, weight, weights,
    psi_t, coef, halo, wide, first, done, out_t, gather, block, sums, pair_out, pair_in,
    load_sem, psi_send, psi_recv, weight_send, weight_recv,
    gather_send, gather_recv, out_send, out_recv, sum_send, sum_recv, pair_send, pair_recv,
):
    band, core, dy = lax.axis_index("band"), lax.axis_index("dx"), lax.axis_index("dy")
    nb = psi_ref.shape[0]
    half = nb // 2
    chunk = half // CHUNKS
    ny = psi_ref.shape[2]
    per = ny // n_band
    other = 1 - core
    up, down = lax.rem(dy + 1, n_dy), lax.rem(dy + n_dy - 1, n_dy)

    barrier = pltpu.get_barrier_semaphore()
    plane = [(i, h) for i in range(n_band) for h in range(2) if i or h]
    chips = [(i, k) for i in range(n_band) for k in range(n_dy) if i or k]
    peers = [(i, h, 0) for i, h in plane]
    peers += [(0, h, k) for h in range(2) for k in (1, n_dy - 1)]

    def at_band(i):
        return lax.rem(band + i, n_band)

    def at_dy(i):
        return lax.rem(dy + i, n_dy)

    def at_core(h):
        return lax.rem(core + h, 2)

    for i, h, k in peers:
        pl.semaphore_signal(
            barrier, inc=1, device_id=(at_band(i), at_core(h), at_dy(k)), device_id_type=MESH
        )
    loads = [
        pltpu.make_async_copy(src, dst, load_sem.at[index])
        for index, (src, dst) in enumerate(
            ((psi_hbm, psi_ref), (level_hbm, level_ref), (site_hbm, site_ref), (base_hbm, base_ref))
        )
    ]
    for load in loads:
        load.start()
    for load in loads:
        load.wait()

    site = site_ref[...]
    picked = jnp.zeros(site.shape, jnp.float32)
    for level in range(level_ref.shape[0]):
        picked = picked + jnp.where(site == level, level_ref[level], jnp.float32(0.0))
    weight[...] = (
        base_ref[...] + picked - (1.5 * SELF_WEIGHT + FILTER_CENTER)
    ) * (1.0 / FILTER_HALF)
    for x in range(2):
        psi_t[x] = jnp.transpose(psi_ref[:, x].astype(jnp.float32), (1, 0, 2)).astype(jnp.bfloat16)

    pl.semaphore_wait(barrier, len(peers))

    layers = pl.ds(2 * core, 2)

    def send(src, dst, send_sem, recv_sem, device):
        copy = pltpu.make_async_remote_copy(
            src_ref=src, dst_ref=dst, send_sem=send_sem, recv_sem=recv_sem,
            device_id=device, device_id_type=MESH,
        )
        copy.start()
        return copy

    routes = [
        (other, dy, 0, 4, ny),
        (core, up, ny - 4, 0, 4), (other, up, ny - 4, 0, 4),
        (core, down, 0, ny + 4, 4), (other, down, 0, ny + 4, 4),
    ]
    potentials, fields = [], []
    for g in range(CHUNKS):
        fields.append([])
        for index, (where, target, from_row, to_row, rows) in enumerate(routes):
            device = (band, where, target)
            bands = pl.ds(pl.multiple_of(where * half + g * chunk, chunk), chunk)
            if g == 0:
                potentials.append(send(
                    weight, weights.at[index],
                    weight_send.at[index], weight_recv.at[index], device,
                ))
            fields[g].append(send(
                psi_t.at[:, pl.ds(from_row, rows), bands],
                halo.at[layers, pl.ds(to_row, rows), pl.ds(g * chunk, chunk)],
                psi_send.at[5 * g + index], psi_recv.at[5 * g + index], device,
            ))

    own = pl.ds(pl.multiple_of(core * half, half), half)
    for x in range(2):
        for y in range(ny):
            coef[2 * core + x, 2 + y] = jnp.broadcast_to(weight[x, y : y + 1], (8, 128))
            wide[2 * core + x, 4 + y] = psi_t[x, y, own].astype(jnp.float32)

    potentials[0].wait()
    for x in range(2):
        for y in range(ny):
            coef[2 * other + x, 2 + y] = jnp.broadcast_to(weights[0, x, y : y + 1], (8, 128))

    def inner(g):
        part = pl.ds(g * chunk, chunk)
        fields[g][0].wait()
        for x in range(2):
            for y in range(ny):
                wide[2 * other + x, 4 + y, part] = halo[2 * other + x, 4 + y, part].astype(jnp.float32)
        over(4, ny, step_one, part)

    def step_one(part, j):
        for x in range(4):
            value = apply_filter(lambda a, r: wide[a, r, part], x, j + 2, coef[x, j])
            first[x, j, part] = value.astype(jnp.bfloat16).astype(jnp.float32)

    def step_two(part, y):
        for x in range(4):
            value = apply_filter(lambda a, r: first[a, r, part], x, y + 2, coef[x, y + 2])
            done[x, y, part] = (2.0 * value - wide[x, y + 4, part]).astype(jnp.bfloat16)

    def widen(part, j):
        for x in range(4):
            wide[x, j, part] = halo[x, j, part].astype(jnp.float32)
            wide[x, ny + 4 + j, part] = halo[x, ny + 4 + j, part].astype(jnp.float32)

    for g in range(CHUNKS):
        inner(g)
    for copy in potentials[1:]:
        copy.wait()
    for index, source, row, to in (
        (1, core, ny - 2, 0), (2, other, ny - 2, 0), (3, core, 0, ny + 2), (4, other, 0, ny + 2)
    ):
        for x in range(2):
            for y in range(2):
                coef[2 * source + x, to + y] = jnp.broadcast_to(
                    weights[index, x, row + y : row + y + 1], (8, 128)
                )

    copies = []
    for g in range(CHUNKS):
        part = pl.ds(g * chunk, chunk)
        for copy in fields[g][1:]:
            copy.wait()
        over(0, 4, widen, part)
        over(0, 4, step_one, part)
        over(ny, ny + 4, step_one, part)
        over(0, ny, step_two, part)
        mine = pl.ds(pl.multiple_of(band * nb + core * half + g * chunk, chunk), chunk)
        for index, (i, h) in enumerate(plane):
            slot = len(plane) * g + index
            copies.append(send(
                done.at[pl.ds(2 * at_core(h), 2), pl.ds(at_band(i) * per, per), part],
                gather.at[:, :, mine],
                gather_send.at[slot], gather_recv.at[slot],
                (at_band(i), at_core(h), dy),
            ))
        for x in range(2):
            for y in range(per):
                gather[x, y, mine] = done[2 * core + x, band * per + y, part]
    out_copy = send(
        done.at[pl.ds(2 * other, 2)], out_t.at[:, :, own],
        out_send.at[0], out_recv.at[0], (band, other, dy),
    )
    for x in range(2):
        for y in range(ny):
            out_t[x, y, own] = done[2 * core + x, y]
    for copy in copies:
        copy.wait()

    total = None
    for x in range(2):
        cells = jnp.concatenate([gather[x, y] for y in range(per)], axis=1)
        term = lax.dot_general(
            cells, cells, (((1,), (1,)), ((), ())), preferred_element_type=jnp.float32
        )
        total = term if total is None else total + term
    low = lax.broadcasted_iota(jnp.int32, (half, 128), 1) < 64
    for i in range(n_band):
        for k in range(n_dy // 2):
            tile = total[nb * i : nb * i + nb, 128 * k : 128 * k + 128]
            top, bottom = tile[:half], tile[half:]
            block[i, 2 * k] = jnp.where(low, top, pltpu.roll(bottom, 64, 1)).astype(jnp.bfloat16)
            block[i, 2 * k + 1] = jnp.where(low, pltpu.roll(top, 64, 1), bottom).astype(jnp.bfloat16)
    here = dy * n_band + band
    copies = []
    for index in range(len(chips)):
        there = index + (here <= index).astype(jnp.int32)
        to_band, to_dy = lax.rem(there, n_band), lax.div(there, n_band)
        send(
            block.at[to_band, to_dy], sums.at[here], sum_send.at[there], sum_recv.at[here],
            (to_band, core, to_dy),
        )
        copies.append(pltpu.make_async_remote_copy(
            src_ref=block.at[to_band, to_dy], dst_ref=sums.at[there],
            send_sem=sum_send.at[there], recv_sem=sum_recv.at[there],
            device_id=(to_band, core, to_dy), device_id_type=MESH,
        ))
    out_copy.wait()
    for x in range(2):
        out_ref[:, x] = jnp.transpose(out_t[x].astype(jnp.float32), (1, 0, 2)).astype(jnp.bfloat16)
    sums[here] = block[band, dy]
    for copy in copies:
        copy.wait()
    result = sums[0].astype(jnp.float32)
    for index in range(1, len(chips) + 1):
        result = result + sums[index].astype(jnp.float32)
    pair_out[...] = result
    copy = send(pair_out, pair_in, pair_send.at[0], pair_recv.at[0], (band, other, dy))
    copy.wait()
    result = (result + pair_in[...]) * (1.0 / cells_all)
    corr_ref[pl.ds(0, half), :] = result[:, :64]
    corr_ref[pl.ds(half, half), :] = pltpu.roll(result, 64, 1)[:, :64]


def store(filtered, correlation, filtered_hbm, correlation_hbm, sem):
    pairs = ((correlation, correlation_hbm), (filtered, filtered_hbm))
    copies = [pltpu.make_async_copy(a, b, sem.at[i]) for i, (a, b) in enumerate(pairs)]
    for copy in copies:
        copy.start()
    for copy in copies:
        copy.wait()


def fused(psi, base_potential, defect_site, defect_level):
    nb, nx, ny, nz = psi.shape
    n_band, n_dy = lax.axis_size("band"), lax.axis_size("dy")
    half, per = nb // 2, ny // n_band
    cells_all = nx * ny * nz * 2 * n_dy
    dma = pltpu.SemaphoreType.DMA
    n_plane, n_chips = 2 * n_band - 1, n_band * n_dy - 1
    vmem = pl.BlockSpec(memory_space=pltpu.VMEM)
    hbm = pl.BlockSpec(memory_space=pltpu.HBM)
    packed = (half, 128)
    filtered, correlation = pl.pallas_call(
        functools.partial(kernel, n_band, n_dy, cells_all),
        out_shape=(
            pltpu.VMEM(psi.shape, jnp.bfloat16),
            pltpu.VMEM((nb, nb * n_band // n_dy), jnp.float32),
        ),
        in_specs=[hbm, hbm, hbm, hbm],
        out_specs=(vmem, vmem),
        scratch_shapes=[
            pltpu.SMEM(defect_level.shape, jnp.float32),
            pltpu.VMEM(psi.shape, jnp.bfloat16),
            pltpu.VMEM(base_potential.shape, jnp.float32),
            pltpu.VMEM(defect_site.shape, jnp.int32),
            pltpu.VMEM(base_potential.shape, jnp.float32),
            pltpu.VMEM((5,) + base_potential.shape, jnp.float32),
            pltpu.VMEM((nx, ny, nb, nz), jnp.bfloat16),
            pltpu.VMEM((2 * nx, ny + 4, 8, nz), jnp.float32),
            pltpu.VMEM((2 * nx, ny + 8, half, nz), jnp.bfloat16),
            pltpu.VMEM((2 * nx, ny + 8, half, nz), jnp.float32),
            pltpu.VMEM((2 * nx, ny + 4, half, nz), jnp.float32),
            pltpu.VMEM((2 * nx, ny, half, nz), jnp.bfloat16),
            pltpu.VMEM((nx, ny, nb, nz), jnp.bfloat16),
            pltpu.VMEM((nx, per, nb * n_band, nz), jnp.bfloat16),
            pltpu.VMEM((n_band, n_dy) + packed, jnp.bfloat16),
            pltpu.VMEM((n_chips + 1,) + packed, jnp.bfloat16),
            pltpu.VMEM(packed, jnp.float32),
            pltpu.VMEM(packed, jnp.float32),
            dma((4,)), dma((5 * CHUNKS,)), dma((5 * CHUNKS,)), dma((5,)), dma((5,)),
            dma((n_plane * CHUNKS,)), dma((n_plane * CHUNKS,)), dma((1,)), dma((1,)),
            dma((n_chips + 1,)), dma((n_chips + 1,)), dma((1,)), dma((1,)),
        ],
        compiler_params=pltpu.CompilerParams(
            collective_id=0, has_side_effects=True, vmem_limit_bytes=64 * 1024 * 1024 - 400 * 1024
        ),
    )(defect_level, psi, base_potential, defect_site)
    return pl.pallas_call(
        store,
        out_shape=(
            jax.ShapeDtypeStruct(filtered.shape, filtered.dtype),
            jax.ShapeDtypeStruct(correlation.shape, correlation.dtype),
        ),
        in_specs=[vmem, vmem],
        out_specs=(hbm, hbm),
        scratch_shapes=[dma((2,))],
    )(*(pltpu.with_memory_space_constraint(a, pltpu.VMEM) for a in (filtered, correlation)))


def solution(mesh):
    in_specs = (P("band", "dx", "dy", None), P("dx", "dy", None), P("dx", "dy", None), P())
    out_specs = (P("band", "dx", "dy", None), P("band", "dy"))
    n_band, n_dx, n_dy = mesh.shape["band"], mesh.shape["dx"], mesh.shape["dy"]

    def body(psi, base_potential, defect_site, defect_level):
        nb, nx, ny, nz = psi.shape
        fits = (
            n_dx == 2 and nx == 2 and nz == 128 and nb == 64
            and n_dy > 2 and nb * n_band == 64 * n_dy and ny % n_band == 0 and ny >= 4
            and n_dy % 2 == 0
        )
        run = fused if fits else shards
        return run(psi, base_potential, defect_site, defect_level)

    return jax.shard_map(body, mesh=mesh, in_specs=in_specs, out_specs=out_specs, check_vma=False)
```

```python
import functools

import jax
import jax.numpy as jnp
from jax import lax
from jax.experimental import pallas as pl
from jax.experimental.pallas import tpu as pltpu
from jax.sharding import PartitionSpec as P

SELF_WEIGHT = -2.5
NEAR_WEIGHT = 4.0 / 3.0
FAR_WEIGHT = -1.0 / 12.0
FILTER_CENTER = 5.5
FILTER_HALF = 3.5


def with_halo(block, sides, width):
    for axis, dim in sides:
        count = lax.axis_size(axis)
        forward = [(i, i + 1) for i in range(count - 1)]
        forward.append((count - 1, 0))
        backward = [(target, source) for source, target in forward]
        low = lax.ppermute(
            lax.slice_in_dim(block, block.shape[dim] - width, None, axis=dim), axis, forward
        )
        high = lax.ppermute(lax.slice_in_dim(block, 0, width, axis=dim), axis, backward)
        block = jnp.concatenate([low, block, high], axis=dim)
    return block


def hamiltonian(field, potential):
    padded = with_halo(field, (("dx", 1), ("dy", 2)), 2).astype(jnp.float32)
    width_x = field.shape[1]
    width_y = field.shape[2]
    center = padded[:, 2 : 2 + width_x, 2 : 2 + width_y, :]
    laplace = 3.0 * SELF_WEIGHT * center
    laplace = laplace + NEAR_WEIGHT * (
        padded[:, 3 : 3 + width_x, 2 : 2 + width_y, :]
        + padded[:, 1 : 1 + width_x, 2 : 2 + width_y, :]
    )
    laplace = laplace + FAR_WEIGHT * (
        padded[:, 4 : 4 + width_x, 2 : 2 + width_y, :] + padded[:, 0:width_x, 2 : 2 + width_y, :]
    )
    laplace = laplace + NEAR_WEIGHT * (
        padded[:, 2 : 2 + width_x, 3 : 3 + width_y, :]
        + padded[:, 2 : 2 + width_x, 1 : 1 + width_y, :]
    )
    laplace = laplace + FAR_WEIGHT * (
        padded[:, 2 : 2 + width_x, 4 : 4 + width_y, :] + padded[:, 2 : 2 + width_x, 0:width_y, :]
    )
    laplace = laplace + NEAR_WEIGHT * (jnp.roll(center, 1, 3) + jnp.roll(center, -1, 3))
    laplace = laplace + FAR_WEIGHT * (jnp.roll(center, 2, 3) + jnp.roll(center, -2, 3))
    return (-0.5 * laplace + potential[None] * center, center)


def shards(psi, base_potential, defect_site, defect_level):
    levels = jnp.arange(defect_level.shape[0], dtype=jnp.int32)
    picked = jnp.sum(
        jnp.where(
            defect_site[None] == levels[:, None, None, None],
            defect_level[:, None, None, None],
            jnp.float32(0.0),
        ),
        axis=0,
    )
    potential = base_potential + picked
    applied, start_field = hamiltonian(psi, potential)
    first = ((applied - FILTER_CENTER * start_field) / FILTER_HALF).astype(jnp.bfloat16)
    applied_next, first_wide = hamiltonian(first, potential)
    filtered = (
        2.0 * (applied_next - FILTER_CENTER * first_wide) / FILTER_HALF - start_field
    ).astype(jnp.bfloat16)
    nb_dev = psi.shape[0]
    cells_all = (
        psi.shape[1] * psi.shape[2] * psi.shape[3] * lax.axis_size("dx") * lax.axis_size("dy")
    )
    flat = filtered.reshape(nb_dev, -1)
    tile = lax.dot_general(
        flat,
        lax.all_gather(flat, "band", axis=0, tiled=True),
        (((1,), (1,)), ((), ())),
        preferred_element_type=jnp.float32,
    )
    column_part = lax.psum_scatter(
        tile.astype(jnp.bfloat16), "dy", scatter_dimension=1, tiled=True
    ).astype(jnp.float32)
    columns = lax.psum(column_part, "dx")
    correlation = columns / cells_all
    return (filtered, correlation)


MESH = pl.DeviceIdType.MESH
CHUNKS = 2


def apply_filter(load, x, j, coef):
    center = load(x, j)
    near = load((x + 1) % 4, j) + load((x + 3) % 4, j)
    far_x = load((x + 2) % 4, j)
    far = far_x + far_x
    near = near + load(x, j + 1) + load(x, j - 1)
    far = far + load(x, j + 2) + load(x, j - 2)
    near = near + pltpu.roll(center, 1, 1) + pltpu.roll(center, 127, 1)
    far = far + pltpu.roll(center, 2, 1) + pltpu.roll(center, 126, 1)
    rows = center.shape[0]
    scaled = (center.reshape(rows // 8, 8, 128) * coef[None]).reshape(rows, 128)
    return (
        scaled
        + near * (-0.5 * NEAR_WEIGHT / FILTER_HALF)
        + far * (-0.5 * FAR_WEIGHT / FILTER_HALF)
    )


def over(low, count, body, part):
    group = next(size for size in (8, 4, 2, 1) if count % size == 0)

    def step(i, carry):
        for k in range(group):
            body(part, low + i * group + k)
        return carry

    lax.fori_loop(0, count // group, step, 0)


def kernel(
    n_band, n_dy, cells_all,
    level_hbm, psi_hbm, base_hbm, site_hbm,
    out_ref, corr_ref,
    level_ref, psi_ref, base_ref, site_ref, weight, weight_in, edge, edge_in,
    psi_t, coef, halo, wide, first, done, out_t, gather, block, own_block, sums, pair_out, pair_in,
    load_sem, pair_psi_send, pair_psi_recv, psi_send, psi_recv, weight_send, weight_recv,
    edge_send, edge_recv, gather_send, gather_recv, out_send, out_recv, sum_send, sum_recv,
    pair_send, pair_recv, greeted,
):
    band, core, dy = lax.axis_index("band"), lax.axis_index("dx"), lax.axis_index("dy")
    nb = psi_ref.shape[0]
    half = nb // 2
    chunk = half // CHUNKS
    ny = psi_ref.shape[2]
    other = 1 - core
    side_a = (dy < n_dy // 2).astype(jnp.int32)
    side_b = 1 - side_a
    inner = dy + 2 * side_a - 1
    outer = lax.rem(dy - 2 * side_a + 1 + n_dy, n_dy)

    barrier = pltpu.get_barrier_semaphore()

    def signal(semaphore, device):
        pl.semaphore_signal(semaphore, inc=1, device_id=device, device_id_type=MESH)

    loads = [
        pltpu.make_async_copy(src, dst, load_sem.at[index])
        for index, (src, dst) in enumerate(
            ((psi_hbm, psi_ref), (level_hbm, level_ref), (site_hbm, site_ref), (base_hbm, base_ref))
        )
    ]
    for load in loads:
        load.start()
    last = dy == n_dy - 1
    for h in range(2):
        signal(barrier, (band, h, inner))
    signal(barrier, (band, other, dy))

    @pl.when(jnp.logical_not(last))
    def _():
        for h in range(2):
            signal(barrier, (band, h, outer))
        for i in range(1, n_band):
            for h in range(2):
                signal(barrier, (lax.rem(band + i, n_band), h, dy))

    for load in loads:
        load.wait()

    site = site_ref[...]
    picked = jnp.zeros(site.shape, jnp.float32)
    for level in range(level_ref.shape[0]):
        picked = picked + jnp.where(site == level, level_ref[level], jnp.float32(0.0))
    weight[...] = (
        base_ref[...] + picked - (1.5 * SELF_WEIGHT + FILTER_CENTER)
    ) * (1.0 / FILTER_HALF)
    for x in range(2):
        edge[0, 2 * x : 2 * x + 2] = weight[x, ny - 2 : ny]
        edge[1, 2 * x : 2 * x + 2] = weight[x, 0:2]
    for x in range(2):
        psi_t[x] = jnp.transpose(psi_ref[:, x].astype(jnp.float32), (1, 0, 2)).astype(jnp.bfloat16)

    @pl.when(dy == 0)
    def _():
        pl.semaphore_wait(barrier, 2 * n_band + 1)

    @pl.when(last)
    def _():
        pl.semaphore_wait(barrier, 5)
        signal(greeted.at[0], (band, core, 0))

    @pl.when(jnp.logical_and(dy > 0, jnp.logical_not(last)))
    def _():
        pl.semaphore_wait(barrier, 2 * n_band + 3)


    layers = pl.ds(2 * core, 2)

    def copy_of(src, dst, send_sem, recv_sem, device):
        return pltpu.make_async_remote_copy(
            src_ref=src, dst_ref=dst, send_sem=send_sem, recv_sem=recv_sem,
            device_id=device, device_id_type=MESH,
        )

    def send(*args):
        copy = copy_of(*args)
        copy.start()
        return copy

    def bands(where, g):
        return pl.ds(pl.multiple_of(where * half + g * chunk, chunk), chunk)

    def part_of(g):
        return pl.ds(g * chunk, chunk)

    def halo_copy(side, target, g, h):
        slot = (side * CHUNKS + g) * 2
        return copy_of(
            psi_t.at[:, pl.ds((1 - side) * (ny - 4), 4), bands(h, g)],
            halo.at[layers, pl.ds(side * (ny + 4), 4), part_of(g)],
            psi_send.at[slot + h], psi_recv.at[slot + core], (band, h, target),
        )

    def edge_copy(side, target, h):
        return copy_of(
            edge.at[side], edge_in.at[side, core],
            edge_send.at[2 * side + h], edge_recv.at[2 * side + core], (band, h, target),
        )

    def send_part(g, side, target):
        for h in range(2):
            if g == 0:
                edge_copy(side, target, h).start()
            halo_copy(side, target, g, h).start()

    def send_side(side, target):
        for g in range(CHUNKS):
            send_part(g, side, target)

    pairs = [
        send(
            psi_t.at[:, :, bands(other, g)], halo.at[layers, pl.ds(4, ny), part_of(g)],
            pair_psi_send.at[g], pair_psi_recv.at[g], (band, other, dy),
        )
        for g in range(CHUNKS)
    ]
    potential = send(
        weight, weight_in, weight_send.at[0], weight_recv.at[0], (band, other, dy)
    )
    @pl.when(dy == 0)
    def _():
        send_side(side_b, inner)
        pl.semaphore_wait(greeted.at[0], 1)
        send_side(side_a, outer)

    @pl.when(dy > 0)
    def _():
        for g in range(CHUNKS):
            for side, target in ((side_b, inner), (side_a, outer)):
                send_part(g, side, target)

    @pl.when(dy == n_dy - 2)
    def _():
        for i in range(1, n_band):
            signal(greeted.at[0], (lax.rem(band + i, n_band), core, dy))
        pl.semaphore_wait(greeted.at[0], n_band - 1)
        signal(greeted.at[0], (band, core, dy + 1))

    own = pl.ds(pl.multiple_of(core * half, half), half)
    for x in range(2):
        for y in range(ny):
            coef[2 * core + x, 2 + y] = jnp.broadcast_to(weight[x, y : y + 1], (8, 128))
            wide[2 * core + x, 4 + y] = psi_t[x, y, own].astype(jnp.float32)

    potential.wait()
    for x in range(2):
        for y in range(ny):
            coef[2 * other + x, 2 + y] = jnp.broadcast_to(weight_in[x, y : y + 1], (8, 128))

    def step_one(part, j):
        for x in range(4):
            value = apply_filter(lambda a, r: wide[a, r, part], x, j + 2, coef[x, j])
            first[x, j, part] = value.astype(jnp.bfloat16).astype(jnp.float32)

    def step_two(part, y):
        for x in range(4):
            value = apply_filter(lambda a, r: first[a, r, part], x, y + 2, coef[x, y + 2])
            done[x, y, part] = (2.0 * value - wide[x, y + 4, part]).astype(jnp.bfloat16)

    def widen(part, j):
        for x in range(4):
            wide[x, j, part] = halo[x, j, part].astype(jnp.float32)

    for g in range(CHUNKS):
        part = part_of(g)
        pairs[g].wait()
        for x in range(2):
            for y in range(ny):
                wide[2 * other + x, 4 + y, part] = halo[2 * other + x, 4 + y, part].astype(jnp.float32)
        over(4, ny - 4, step_one, part)

    me = 2 * band + core
    def row_of(side, i):
        return side * (ny // 2) + i

    def out_copy(stage, g):
        rows = pl.ds(sides[stage] * (ny // 2), ny // 2)
        place = pl.ds(pl.multiple_of(core * half + g * chunk, chunk), chunk)
        return copy_of(
            done.at[pl.ds(2 * other, 2), rows, part_of(g)], out_t.at[:, rows, place],
            out_send.at[stage * CHUNKS + g], out_recv.at[stage * CHUNKS + g], (band, other, dy),
        )

    def gather_copy(stage, g, i, h):
        place = pl.ds(pl.multiple_of(band * nb + core * half + g * chunk, chunk), chunk)
        slot = stage * CHUNKS + g
        return copy_of(
            done.at[pl.ds(2 * h, 2), row_of(sides[stage], i), part_of(g)],
            gather.at[:, stage, place],
            gather_send.at[(i * 2 + h) * 2 * CHUNKS + slot], gather_recv.at[me * 2 * CHUNKS + slot],
            (i, h, dy),
        )

    sides = (side_a, side_b)

    @pl.when(last)
    def _():
        pl.semaphore_wait(greeted.at[0], 1)

    for stage, side in enumerate(sides):
        for g in range(CHUNKS):
            part = part_of(g)
            if g == 0:
                for h in range(2):
                    copy_of(
                        edge.at[side], edge_in.at[side, h],
                        edge_send.at[2 * side + h], edge_recv.at[2 * side + h], (band, h, inner),
                    ).wait_recv()
                for source in range(2):
                    for x in range(2):
                        for y in range(2):
                            coef[2 * source + x, side * (ny + 2) + y] = jnp.broadcast_to(
                                edge_in[side, source, 2 * x + y : 2 * x + y + 1], (8, 128)
                            )
            for h in range(2):
                slot = (side * CHUNKS + g) * 2 + h
                copy_of(
                    psi_t.at[:, pl.ds(0, 4), bands(h, g)],
                    halo.at[pl.ds(2 * h, 2), pl.ds(side * (ny + 4), 4), part],
                    psi_send.at[slot], psi_recv.at[slot], (band, h, inner),
                ).wait_recv()
            over(side * (ny + 4), 4, widen, part)
            over(side * ny, 4, step_one, part)
            over(side * (ny // 2), ny // 2, step_two, part)
            for i in range(n_band):
                for h in range(2):

                    @pl.when(me != 2 * i + h)
                    def _():
                        gather_copy(stage, g, i, h).start()

            out_copy(stage, g).start()

    for g in range(CHUNKS):
        place = pl.ds(pl.multiple_of(band * nb + core * half + g * chunk, chunk), chunk)
        for x in range(2):
            for stage in range(2):
                gather[x, stage, place] = done[2 * core + x, row_of(sides[stage], band), part_of(g)]
    for x in range(2):
        for y in range(ny):
            out_t[x, y, own] = done[2 * core + x, y]
    for stage in range(2):
        for g in range(CHUNKS):
            out_copy(stage, g).wait()

    def pack(tile):
        top, bottom = tile[:half], tile[half:]
        return (
            jnp.where(low, top, pltpu.roll(bottom, 64, 1)).astype(jnp.bfloat16),
            jnp.where(low, pltpu.roll(top, 64, 1), bottom).astype(jnp.bfloat16),
        )

    low = lax.broadcasted_iota(jnp.int32, (half, 128), 1) < 64
    cells = jnp.concatenate([out_t[x, y] for x in range(2) for y in range(ny)], axis=1)
    square = lax.dot_general(
        cells, cells, (((1,), (1,)), ((), ())), preferred_element_type=jnp.float32
    )
    square = jnp.concatenate([square, square], axis=1)
    own_block[...] = jnp.where(low, square[:half], square[half:]).astype(jnp.bfloat16)

    def own_copy(slot):
        return copy_of(
            own_block, sums.at[slot * n_band + band],
            sum_send.at[band * n_band + band], sum_recv.at[slot * n_band + band],
            (band, core, band),
        )

    @pl.when(dy != band)
    def _():
        own_copy(dy).start()

    for j in range(1, 2 * n_band):
        source = lax.rem(me + j, 2 * n_band)
        for g in range(CHUNKS):
            place = pl.ds(pl.multiple_of(source * half + g * chunk, chunk), chunk)
            for stage in range(2):
                slot = source * 2 * CHUNKS + stage * CHUNKS + g
                copy_of(
                    gather.at[:, stage, place], gather.at[:, stage, place],
                    gather_send.at[slot], gather_recv.at[slot],
                    (lax.div(source, 2), lax.rem(source, 2), dy),
                ).wait_recv()

    total = None
    for x in range(2):
        cells = jnp.concatenate([gather[x, y] for y in range(2)], axis=1)
        term = lax.dot_general(
            cells, cells, (((1,), (1,)), ((), ())), preferred_element_type=jnp.float32
        )
        total = term if total is None else total + term
    for i in range(n_band):
        for k in range(n_dy // 2):
            tile = total[nb * i : nb * i + nb, 128 * k : 128 * k + 128]
            block[i, 2 * k], block[i, 2 * k + 1] = pack(tile)
    here = dy * n_band + band
    n_chips = n_band * n_dy

    def sum_copy(there, slot):
        to_band, to_dy = there % n_band, there // n_band
        return copy_of(
            block.at[to_band, to_dy], sums.at[slot], sum_send.at[there], sum_recv.at[slot],
            (to_band, core, to_dy),
        )

    targets = [t for t in range(n_chips) if t % n_band != t // n_band]
    for there in targets:

        @pl.when(there != here)
        def _():
            sum_copy(there, here).start()

    for x in range(2):
        out_ref[:, x] = jnp.transpose(out_t[x].astype(jnp.float32), (1, 0, 2)).astype(jnp.bfloat16)
    for side in range(2):
        for h in range(2):
            edge_copy(side, inner, h).wait_send()
            for g in range(CHUNKS):
                halo_copy(side, inner, g, h).wait_send()
    for i in range(n_band):
        for h in range(2):

            @pl.when(me != 2 * i + h)
            def _():
                for stage in range(2):
                    for g in range(CHUNKS):
                        gather_copy(stage, g, i, h).wait_send()

    def landed(slot):
        copy_of(
            own_block, sums.at[slot], sum_send.at[slot], sum_recv.at[slot], (band, other, dy)
        ).wait_recv()

    @pl.when(dy == band)
    def _():
        result = own_block[...].astype(jnp.float32)
        for j in range(1, n_dy):
            slot = lax.rem(dy + j, n_dy) * n_band + band
            landed(slot)
            result = result + sums[slot].astype(jnp.float32)
        pair_out[...] = result

    @pl.when(dy != band)
    def _():
        own_copy(dy).wait_send()
        result = block[band, dy].astype(jnp.float32)
        for j in range(1, n_chips):
            slot = lax.rem(here + j, n_chips)
            landed(slot)
            result = result + sums[slot].astype(jnp.float32)
        pair_out[...] = result

    result = pair_out[...]
    copy = send(pair_out, pair_in, pair_send.at[0], pair_recv.at[0], (band, other, dy))
    copy.wait()
    for there in targets:

        @pl.when(there != here)
        def _():
            sum_copy(there, here).wait_send()

    result = (result + pair_in[...]) * (1.0 / cells_all)
    corr_ref[pl.ds(0, half), :] = result[:, :64]
    corr_ref[pl.ds(half, half), :] = pltpu.roll(result, 64, 1)[:, :64]


def store(filtered, correlation, filtered_hbm, correlation_hbm, sem):
    pairs = ((correlation, correlation_hbm), (filtered, filtered_hbm))
    copies = [pltpu.make_async_copy(a, b, sem.at[i]) for i, (a, b) in enumerate(pairs)]
    for copy in copies:
        copy.start()
    for copy in copies:
        copy.wait()


def fused(psi, base_potential, defect_site, defect_level):
    nb, nx, ny, nz = psi.shape
    n_band, n_dy = lax.axis_size("band"), lax.axis_size("dy")
    half, per = nb // 2, ny // n_band
    cells_all = nx * ny * nz * 2 * n_dy
    dma = pltpu.SemaphoreType.DMA
    n_plane, n_chips = 2 * n_band, n_band * n_dy
    vmem = pl.BlockSpec(memory_space=pltpu.VMEM)
    hbm = pl.BlockSpec(memory_space=pltpu.HBM)
    packed = (half, 128)
    filtered, correlation = pl.pallas_call(
        functools.partial(kernel, n_band, n_dy, cells_all),
        out_shape=(
            pltpu.VMEM(psi.shape, jnp.bfloat16),
            pltpu.VMEM((nb, nb * n_band // n_dy), jnp.float32),
        ),
        in_specs=[hbm, hbm, hbm, hbm],
        out_specs=(vmem, vmem),
        scratch_shapes=[
            pltpu.SMEM(defect_level.shape, jnp.float32),
            pltpu.VMEM(psi.shape, jnp.bfloat16),
            pltpu.VMEM(base_potential.shape, jnp.float32),
            pltpu.VMEM(defect_site.shape, jnp.int32),
            pltpu.VMEM(base_potential.shape, jnp.float32),
            pltpu.VMEM(base_potential.shape, jnp.float32),
            pltpu.VMEM((2, 4, nz), jnp.float32),
            pltpu.VMEM((2, 2, 4, nz), jnp.float32),
            pltpu.VMEM((nx, ny, nb, nz), jnp.bfloat16),
            pltpu.VMEM((2 * nx, ny + 4, 8, nz), jnp.float32),
            pltpu.VMEM((2 * nx, ny + 8, half, nz), jnp.bfloat16),
            pltpu.VMEM((2 * nx, ny + 8, half, nz), jnp.float32),
            pltpu.VMEM((2 * nx, ny + 4, half, nz), jnp.float32),
            pltpu.VMEM((2 * nx, ny, half, nz), jnp.bfloat16),
            pltpu.VMEM((nx, ny, nb, nz), jnp.bfloat16),
            pltpu.VMEM((nx, per, nb * n_band, nz), jnp.bfloat16),
            pltpu.VMEM((n_band, n_dy) + packed, jnp.bfloat16),
            pltpu.VMEM(packed, jnp.bfloat16),
            pltpu.VMEM((n_chips,) + packed, jnp.bfloat16),
            pltpu.VMEM(packed, jnp.float32),
            pltpu.VMEM(packed, jnp.float32),
            dma((4,)), dma((CHUNKS,)), dma((CHUNKS,)), dma((4 * CHUNKS,)), dma((4 * CHUNKS,)),
            dma((1,)), dma((1,)), dma((4,)), dma((4,)),
            dma((2 * n_plane * CHUNKS,)), dma((2 * n_plane * CHUNKS,)),
            dma((2 * CHUNKS,)), dma((2 * CHUNKS,)),
            dma((n_chips,)), dma((n_chips,)), dma((1,)), dma((1,)),
            pltpu.SemaphoreType.REGULAR((1,)),
        ],
        compiler_params=pltpu.CompilerParams(
            collective_id=0, has_side_effects=True, vmem_limit_bytes=64 * 1024 * 1024 - 400 * 1024
        ),
    )(defect_level, psi, base_potential, defect_site)
    return pl.pallas_call(
        store,
        out_shape=(
            jax.ShapeDtypeStruct(filtered.shape, filtered.dtype),
            jax.ShapeDtypeStruct(correlation.shape, correlation.dtype),
        ),
        in_specs=[vmem, vmem],
        out_specs=(hbm, hbm),
        scratch_shapes=[dma((2,))],
    )(*(pltpu.with_memory_space_constraint(a, pltpu.VMEM) for a in (filtered, correlation)))


def solution(mesh):
    in_specs = (P("band", "dx", "dy", None), P("dx", "dy", None), P("dx", "dy", None), P())
    out_specs = (P("band", "dx", "dy", None), P("band", "dy"))
    n_band, n_dx, n_dy = mesh.shape["band"], mesh.shape["dx"], mesh.shape["dy"]

    def body(psi, base_potential, defect_site, defect_level):
        nb, nx, ny, nz = psi.shape
        fits = (
            n_dx == 2 and nx == 2 and nz == 128 and nb == 64
            and n_dy == 4 and n_band == 4 and ny == 8
        )
        run = fused if fits else shards
        return run(psi, base_potential, defect_site, defect_level)

    return jax.shard_map(body, mesh=mesh, in_specs=in_specs, out_specs=out_specs, check_vma=False)
```

```python
import functools

import jax
import jax.numpy as jnp
from jax import lax
from jax.experimental import pallas as pl
from jax.experimental.pallas import tpu as pltpu
from jax.sharding import PartitionSpec as P

SELF_WEIGHT = -2.5
NEAR_WEIGHT = 4.0 / 3.0
FAR_WEIGHT = -1.0 / 12.0
FILTER_CENTER = 5.5
FILTER_HALF = 3.5


def with_halo(block, sides, width):
    for axis, dim in sides:
        count = lax.axis_size(axis)
        forward = [(i, i + 1) for i in range(count - 1)]
        forward.append((count - 1, 0))
        backward = [(target, source) for source, target in forward]
        low = lax.ppermute(
            lax.slice_in_dim(block, block.shape[dim] - width, None, axis=dim), axis, forward
        )
        high = lax.ppermute(lax.slice_in_dim(block, 0, width, axis=dim), axis, backward)
        block = jnp.concatenate([low, block, high], axis=dim)
    return block


def hamiltonian(field, potential):
    padded = with_halo(field, (("dx", 1), ("dy", 2)), 2).astype(jnp.float32)
    width_x = field.shape[1]
    width_y = field.shape[2]
    center = padded[:, 2 : 2 + width_x, 2 : 2 + width_y, :]
    laplace = 3.0 * SELF_WEIGHT * center
    laplace = laplace + NEAR_WEIGHT * (
        padded[:, 3 : 3 + width_x, 2 : 2 + width_y, :]
        + padded[:, 1 : 1 + width_x, 2 : 2 + width_y, :]
    )
    laplace = laplace + FAR_WEIGHT * (
        padded[:, 4 : 4 + width_x, 2 : 2 + width_y, :] + padded[:, 0:width_x, 2 : 2 + width_y, :]
    )
    laplace = laplace + NEAR_WEIGHT * (
        padded[:, 2 : 2 + width_x, 3 : 3 + width_y, :]
        + padded[:, 2 : 2 + width_x, 1 : 1 + width_y, :]
    )
    laplace = laplace + FAR_WEIGHT * (
        padded[:, 2 : 2 + width_x, 4 : 4 + width_y, :] + padded[:, 2 : 2 + width_x, 0:width_y, :]
    )
    laplace = laplace + NEAR_WEIGHT * (jnp.roll(center, 1, 3) + jnp.roll(center, -1, 3))
    laplace = laplace + FAR_WEIGHT * (jnp.roll(center, 2, 3) + jnp.roll(center, -2, 3))
    return (-0.5 * laplace + potential[None] * center, center)


def shards(psi, base_potential, defect_site, defect_level):
    levels = jnp.arange(defect_level.shape[0], dtype=jnp.int32)
    picked = jnp.sum(
        jnp.where(
            defect_site[None] == levels[:, None, None, None],
            defect_level[:, None, None, None],
            jnp.float32(0.0),
        ),
        axis=0,
    )
    potential = base_potential + picked
    applied, start_field = hamiltonian(psi, potential)
    first = ((applied - FILTER_CENTER * start_field) / FILTER_HALF).astype(jnp.bfloat16)
    applied_next, first_wide = hamiltonian(first, potential)
    filtered = (
        2.0 * (applied_next - FILTER_CENTER * first_wide) / FILTER_HALF - start_field
    ).astype(jnp.bfloat16)
    nb_dev = psi.shape[0]
    cells_all = (
        psi.shape[1] * psi.shape[2] * psi.shape[3] * lax.axis_size("dx") * lax.axis_size("dy")
    )
    flat = filtered.reshape(nb_dev, -1)
    tile = lax.dot_general(
        flat,
        lax.all_gather(flat, "band", axis=0, tiled=True),
        (((1,), (1,)), ((), ())),
        preferred_element_type=jnp.float32,
    )
    column_part = lax.psum_scatter(
        tile.astype(jnp.bfloat16), "dy", scatter_dimension=1, tiled=True
    ).astype(jnp.float32)
    columns = lax.psum(column_part, "dx")
    correlation = columns / cells_all
    return (filtered, correlation)


MESH = pl.DeviceIdType.MESH
CHUNKS = 2


def apply_filter(load, x, j, coef):
    center = load(x, j)
    near = load((x + 1) % 4, j) + load((x + 3) % 4, j)
    far_x = load((x + 2) % 4, j)
    far = far_x + far_x
    near = near + load(x, j + 1) + load(x, j - 1)
    far = far + load(x, j + 2) + load(x, j - 2)
    near = near + pltpu.roll(center, 1, 1) + pltpu.roll(center, 127, 1)
    far = far + pltpu.roll(center, 2, 1) + pltpu.roll(center, 126, 1)
    rows = center.shape[0]
    scaled = (center.reshape(rows // 8, 8, 128) * coef[None]).reshape(rows, 128)
    return (
        scaled
        + near * (-0.5 * NEAR_WEIGHT / FILTER_HALF)
        + far * (-0.5 * FAR_WEIGHT / FILTER_HALF)
    )


def over(low, count, body, part):
    group = next(size for size in (8, 4, 2, 1) if count % size == 0)

    def step(i, carry):
        for k in range(group):
            body(part, low + i * group + k)
        return carry

    lax.fori_loop(0, count // group, step, 0)


def kernel(
    n_band, n_dy, cells_all,
    level_hbm, psi_hbm, base_hbm, site_hbm,
    out_ref, corr_ref,
    level_ref, psi_ref, base_ref, site_ref, weight, weight_in, edge, edge_in,
    psi_t, coef, halo, wide, first, done, out_t, gather, block, own_block, sums, pair_out, pair_in,
    load_sem, pair_psi_send, pair_psi_recv, psi_send, psi_recv, weight_send, weight_recv,
    edge_send, edge_recv, gather_send, gather_recv, out_send, out_recv, sum_send, sum_recv,
    pair_send, pair_recv, greeted,
):
    band, core, dy = lax.axis_index("band"), lax.axis_index("dx"), lax.axis_index("dy")
    nb = psi_ref.shape[0]
    half = nb // 2
    chunk = half // CHUNKS
    ny = psi_ref.shape[2]
    other = 1 - core
    side_a = (dy < n_dy // 2).astype(jnp.int32)
    side_b = 1 - side_a
    inner = dy + 2 * side_a - 1
    outer = lax.rem(dy - 2 * side_a + 1 + n_dy, n_dy)

    barrier = pltpu.get_barrier_semaphore()

    def signal(semaphore, device):
        pl.semaphore_signal(semaphore, inc=1, device_id=device, device_id_type=MESH)

    pieces = [pl.ds(h * half + g * chunk, chunk) for g in range(CHUNKS) for h in range(2)]
    loads = [
        pltpu.make_async_copy(src, dst, load_sem.at[index])
        for index, (src, dst) in enumerate(
            [(psi_hbm.at[rows], psi_ref.at[rows]) for rows in pieces]
            + [(level_hbm, level_ref), (site_hbm, site_ref), (base_hbm, base_ref)]
        )
    ]
    for load in loads:
        load.start()
    last = dy == n_dy - 1
    for h in range(2):
        signal(barrier, (band, h, inner))
    signal(barrier, (band, other, dy))

    @pl.when(jnp.logical_not(last))
    def _():
        for h in range(2):
            signal(barrier, (band, h, outer))
        for i in range(1, n_band):
            for h in range(2):
                signal(barrier, (lax.rem(band + i, n_band), h, dy))

    @pl.when(last)
    def _():
        pl.semaphore_wait(barrier, 5)
        signal(greeted.at[0], (band, core, 0))

    for load in loads[2 * CHUNKS :]:
        load.wait()

    site = site_ref[...]
    picked = jnp.zeros(site.shape, jnp.float32)
    for level in range(level_ref.shape[0]):
        picked = picked + jnp.where(site == level, level_ref[level], jnp.float32(0.0))
    weight[...] = (
        base_ref[...] + picked - (1.5 * SELF_WEIGHT + FILTER_CENTER)
    ) * (1.0 / FILTER_HALF)
    for x in range(2):
        edge[0, 2 * x : 2 * x + 2] = weight[x, ny - 2 : ny]
        edge[1, 2 * x : 2 * x + 2] = weight[x, 0:2]

    def turn(g):
        for h in range(2):
            loads[2 * g + h].wait()
            rows = pieces[2 * g + h]
            for x in range(2):
                psi_t[x, :, rows] = jnp.transpose(
                    psi_ref[rows, x].astype(jnp.float32), (1, 0, 2)
                ).astype(jnp.bfloat16)

    turn(0)

    @pl.when(dy == 0)
    def _():
        pl.semaphore_wait(barrier, 2 * n_band + 1)

    @pl.when(jnp.logical_and(dy > 0, jnp.logical_not(last)))
    def _():
        pl.semaphore_wait(barrier, 2 * n_band + 3)


    layers = pl.ds(2 * core, 2)

    def copy_of(src, dst, send_sem, recv_sem, device):
        return pltpu.make_async_remote_copy(
            src_ref=src, dst_ref=dst, send_sem=send_sem, recv_sem=recv_sem,
            device_id=device, device_id_type=MESH,
        )

    def send(*args):
        copy = copy_of(*args)
        copy.start()
        return copy

    def bands(where, g):
        return pl.ds(pl.multiple_of(where * half + g * chunk, chunk), chunk)

    def part_of(g):
        return pl.ds(g * chunk, chunk)

    def halo_copy(side, target, g, h):
        slot = (side * CHUNKS + g) * 2
        return copy_of(
            psi_t.at[:, pl.ds((1 - side) * (ny - 4), 4), bands(h, g)],
            halo.at[layers, pl.ds(side * (ny + 4), 4), part_of(g)],
            psi_send.at[slot + h], psi_recv.at[slot + core], (band, h, target),
        )

    def edge_copy(side, target, h):
        return copy_of(
            edge.at[side], edge_in.at[side, core],
            edge_send.at[2 * side + h], edge_recv.at[2 * side + core], (band, h, target),
        )

    def send_part(g, side, target):
        for h in range(2):
            if g == 0:
                edge_copy(side, target, h).start()
            halo_copy(side, target, g, h).start()

    def send_side(side, target):
        for g in range(CHUNKS):
            send_part(g, side, target)

    @pl.when(dy > 0)
    def _():
        send_part(0, side_b, inner)
        send_part(0, side_a, outer)

    turn(1)

    @pl.when(dy > 0)
    def _():
        send_part(1, side_b, inner)
        send_part(1, side_a, outer)

    pairs = [
        send(
            psi_t.at[:, :, bands(other, g)], halo.at[layers, pl.ds(4, ny), part_of(g)],
            pair_psi_send.at[g], pair_psi_recv.at[g], (band, other, dy),
        )
        for g in range(CHUNKS)
    ]
    potential = send(
        weight, weight_in, weight_send.at[0], weight_recv.at[0], (band, other, dy)
    )

    @pl.when(dy == 0)
    def _():
        send_side(side_b, inner)
        pl.semaphore_wait(greeted.at[0], 1)
        send_side(side_a, outer)

    @pl.when(dy == n_dy - 2)
    def _():
        for i in range(1, n_band):
            signal(greeted.at[0], (lax.rem(band + i, n_band), core, dy))
        pl.semaphore_wait(greeted.at[0], n_band - 1)
        signal(greeted.at[0], (band, core, dy + 1))

    own = pl.ds(pl.multiple_of(core * half, half), half)
    for x in range(2):
        for y in range(ny):
            coef[2 * core + x, 2 + y] = jnp.broadcast_to(weight[x, y : y + 1], (8, 128))
            wide[2 * core + x, 4 + y] = psi_t[x, y, own].astype(jnp.float32)

    potential.wait()
    for x in range(2):
        for y in range(ny):
            coef[2 * other + x, 2 + y] = jnp.broadcast_to(weight_in[x, y : y + 1], (8, 128))

    def step_one(part, j):
        for x in range(4):
            value = apply_filter(lambda a, r: wide[a, r, part], x, j + 2, coef[x, j])
            first[x, j, part] = value.astype(jnp.bfloat16).astype(jnp.float32)

    def step_two(part, y):
        for x in range(4):
            value = apply_filter(lambda a, r: first[a, r, part], x, y + 2, coef[x, y + 2])
            done[x, y, part] = (2.0 * value - wide[x, y + 4, part]).astype(jnp.bfloat16)

    def widen(part, j):
        for x in range(4):
            wide[x, j, part] = halo[x, j, part].astype(jnp.float32)

    for g in range(CHUNKS):
        part = part_of(g)
        pairs[g].wait()
        for x in range(2):
            for y in range(ny):
                wide[2 * other + x, 4 + y, part] = halo[2 * other + x, 4 + y, part].astype(jnp.float32)
        over(4, ny - 4, step_one, part)

    me = 2 * band + core
    def row_of(side, i):
        return side * (ny // 2) + i

    def out_copy(stage, g):
        rows = pl.ds(sides[stage] * (ny // 2), ny // 2)
        place = pl.ds(pl.multiple_of(core * half + g * chunk, chunk), chunk)
        return copy_of(
            done.at[pl.ds(2 * other, 2), rows, part_of(g)], out_t.at[:, rows, place],
            out_send.at[stage * CHUNKS + g], out_recv.at[stage * CHUNKS + g], (band, other, dy),
        )

    def gather_copy(stage, g, i, h):
        place = pl.ds(pl.multiple_of(band * nb + core * half + g * chunk, chunk), chunk)
        slot = stage * CHUNKS + g
        return copy_of(
            done.at[pl.ds(2 * h, 2), row_of(sides[stage], i), part_of(g)],
            gather.at[:, stage, place],
            gather_send.at[(i * 2 + h) * 2 * CHUNKS + slot], gather_recv.at[me * 2 * CHUNKS + slot],
            (i, h, dy),
        )

    sides = (side_a, side_b)

    @pl.when(last)
    def _():
        pl.semaphore_wait(greeted.at[0], 1)

    for stage, side in enumerate(sides):
        for g in range(CHUNKS):
            part = part_of(g)
            if g == 0:
                for h in range(2):
                    copy_of(
                        edge.at[side], edge_in.at[side, h],
                        edge_send.at[2 * side + h], edge_recv.at[2 * side + h], (band, h, inner),
                    ).wait_recv()
                for source in range(2):
                    for x in range(2):
                        for y in range(2):
                            coef[2 * source + x, side * (ny + 2) + y] = jnp.broadcast_to(
                                edge_in[side, source, 2 * x + y : 2 * x + y + 1], (8, 128)
                            )
            for h in range(2):
                slot = (side * CHUNKS + g) * 2 + h
                copy_of(
                    psi_t.at[:, pl.ds(0, 4), bands(h, g)],
                    halo.at[pl.ds(2 * h, 2), pl.ds(side * (ny + 4), 4), part],
                    psi_send.at[slot], psi_recv.at[slot], (band, h, inner),
                ).wait_recv()
            over(side * (ny + 4), 4, widen, part)
            over(side * ny, 4, step_one, part)
            over(side * (ny // 2), ny // 2, step_two, part)
            for i in range(n_band):
                for h in range(2):

                    @pl.when(me != 2 * i + h)
                    def _():
                        gather_copy(stage, g, i, h).start()

            out_copy(stage, g).start()

    for g in range(CHUNKS):
        place = pl.ds(pl.multiple_of(band * nb + core * half + g * chunk, chunk), chunk)
        for x in range(2):
            for stage in range(2):
                gather[x, stage, place] = done[2 * core + x, row_of(sides[stage], band), part_of(g)]
    for x in range(2):
        for y in range(ny):
            out_t[x, y, own] = done[2 * core + x, y]
    for stage in range(2):
        for g in range(CHUNKS):
            out_copy(stage, g).wait()

    def pack(tile):
        top, bottom = tile[:half], tile[half:]
        return (
            jnp.where(low, top, pltpu.roll(bottom, 64, 1)).astype(jnp.bfloat16),
            jnp.where(low, pltpu.roll(top, 64, 1), bottom).astype(jnp.bfloat16),
        )

    low = lax.broadcasted_iota(jnp.int32, (half, 128), 1) < 64
    cells = jnp.concatenate([out_t[x, y] for x in range(2) for y in range(ny)], axis=1)
    square = lax.dot_general(
        cells, cells, (((1,), (1,)), ((), ())), preferred_element_type=jnp.float32
    )
    square = jnp.concatenate([square, square], axis=1)
    own_block[...] = jnp.where(low, square[:half], square[half:]).astype(jnp.bfloat16)

    def own_copy(slot):
        return copy_of(
            own_block, sums.at[slot * n_band + band],
            sum_send.at[band * n_band + band], sum_recv.at[slot * n_band + band],
            (band, core, band),
        )

    @pl.when(dy != band)
    def _():
        own_copy(dy).start()

    for j in range(1, 2 * n_band):
        source = lax.rem(me + j, 2 * n_band)
        for g in range(CHUNKS):
            place = pl.ds(pl.multiple_of(source * half + g * chunk, chunk), chunk)
            for stage in range(2):
                slot = source * 2 * CHUNKS + stage * CHUNKS + g
                copy_of(
                    gather.at[:, stage, place], gather.at[:, stage, place],
                    gather_send.at[slot], gather_recv.at[slot],
                    (lax.div(source, 2), lax.rem(source, 2), dy),
                ).wait_recv()

    total = None
    for x in range(2):
        cells = jnp.concatenate([gather[x, y] for y in range(2)], axis=1)
        term = lax.dot_general(
            cells, cells, (((1,), (1,)), ((), ())), preferred_element_type=jnp.float32
        )
        total = term if total is None else total + term
    for i in range(n_band):
        for k in range(n_dy // 2):
            tile = total[nb * i : nb * i + nb, 128 * k : 128 * k + 128]
            block[i, 2 * k], block[i, 2 * k + 1] = pack(tile)
    here = dy * n_band + band
    n_chips = n_band * n_dy

    def sum_copy(to_band, to_dy):
        return copy_of(
            block.at[to_band, to_dy], sums.at[here], sum_send.at[to_dy * n_band + to_band],
            sum_recv.at[here], (to_band, core, to_dy),
        )

    low_half = (dy < n_dy // 2).astype(jnp.int32)
    targets = [
        (i, low_half * (n_dy - 1 - k) + (1 - low_half) * k) for k in range(n_dy) for i in range(n_band)
    ]

    def each_target(act):
        for to_band, to_dy in targets:
            itself = jnp.logical_and(to_band == band, to_dy == dy)

            @pl.when(jnp.logical_not(jnp.logical_or(itself, to_dy == to_band)))
            def _():
                act(sum_copy(to_band, to_dy))

    each_target(lambda copy: copy.start())

    for x in range(2):
        out_ref[:, x] = jnp.transpose(out_t[x].astype(jnp.float32), (1, 0, 2)).astype(jnp.bfloat16)
    for side in range(2):
        for h in range(2):
            edge_copy(side, inner, h).wait_send()
            for g in range(CHUNKS):
                halo_copy(side, inner, g, h).wait_send()
    for i in range(n_band):
        for h in range(2):

            @pl.when(me != 2 * i + h)
            def _():
                for stage in range(2):
                    for g in range(CHUNKS):
                        gather_copy(stage, g, i, h).wait_send()

    def landed(slot):
        copy_of(
            own_block, sums.at[slot], sum_send.at[slot], sum_recv.at[slot], (band, other, dy)
        ).wait_recv()

    @pl.when(dy == band)
    def _():
        result = own_block[...].astype(jnp.float32)
        for j in range(1, n_dy):
            slot = lax.rem(dy + j, n_dy) * n_band + band
            landed(slot)
            result = result + sums[slot].astype(jnp.float32)
        pair_out[...] = result

    @pl.when(dy != band)
    def _():
        own_copy(dy).wait_send()
        result = block[band, dy].astype(jnp.float32)
        for j in range(1, n_chips):
            slot = lax.rem(here + j, n_chips)
            landed(slot)
            result = result + sums[slot].astype(jnp.float32)
        pair_out[...] = result

    result = pair_out[...]
    copy = send(pair_out, pair_in, pair_send.at[0], pair_recv.at[0], (band, other, dy))
    copy.wait()
    each_target(lambda copy: copy.wait_send())

    result = (result + pair_in[...]) * (1.0 / cells_all)
    corr_ref[pl.ds(0, half), :] = result[:, :64]
    corr_ref[pl.ds(half, half), :] = pltpu.roll(result, 64, 1)[:, :64]


def store(filtered, correlation, filtered_hbm, correlation_hbm, sem):
    pairs = ((correlation, correlation_hbm), (filtered, filtered_hbm))
    copies = [pltpu.make_async_copy(a, b, sem.at[i]) for i, (a, b) in enumerate(pairs)]
    for copy in copies:
        copy.start()
    for copy in copies:
        copy.wait()


def fused(psi, base_potential, defect_site, defect_level):
    nb, nx, ny, nz = psi.shape
    n_band, n_dy = lax.axis_size("band"), lax.axis_size("dy")
    half, per = nb // 2, ny // n_band
    cells_all = nx * ny * nz * 2 * n_dy
    dma = pltpu.SemaphoreType.DMA
    n_plane, n_chips = 2 * n_band, n_band * n_dy
    vmem = pl.BlockSpec(memory_space=pltpu.VMEM)
    hbm = pl.BlockSpec(memory_space=pltpu.HBM)
    packed = (half, 128)
    filtered, correlation = pl.pallas_call(
        functools.partial(kernel, n_band, n_dy, cells_all),
        out_shape=(
            pltpu.VMEM(psi.shape, jnp.bfloat16),
            pltpu.VMEM((nb, nb * n_band // n_dy), jnp.float32),
        ),
        in_specs=[hbm, hbm, hbm, hbm],
        out_specs=(vmem, vmem),
        scratch_shapes=[
            pltpu.SMEM(defect_level.shape, jnp.float32),
            pltpu.VMEM(psi.shape, jnp.bfloat16),
            pltpu.VMEM(base_potential.shape, jnp.float32),
            pltpu.VMEM(defect_site.shape, jnp.int32),
            pltpu.VMEM(base_potential.shape, jnp.float32),
            pltpu.VMEM(base_potential.shape, jnp.float32),
            pltpu.VMEM((2, 4, nz), jnp.float32),
            pltpu.VMEM((2, 2, 4, nz), jnp.float32),
            pltpu.VMEM((nx, ny, nb, nz), jnp.bfloat16),
            pltpu.VMEM((2 * nx, ny + 4, 8, nz), jnp.float32),
            pltpu.VMEM((2 * nx, ny + 8, half, nz), jnp.bfloat16),
            pltpu.VMEM((2 * nx, ny + 8, half, nz), jnp.float32),
            pltpu.VMEM((2 * nx, ny + 4, half, nz), jnp.float32),
            pltpu.VMEM((2 * nx, ny, half, nz), jnp.bfloat16),
            pltpu.VMEM((nx, ny, nb, nz), jnp.bfloat16),
            pltpu.VMEM((nx, per, nb * n_band, nz), jnp.bfloat16),
            pltpu.VMEM((n_band, n_dy) + packed, jnp.bfloat16),
            pltpu.VMEM(packed, jnp.bfloat16),
            pltpu.VMEM((n_chips,) + packed, jnp.bfloat16),
            pltpu.VMEM(packed, jnp.float32),
            pltpu.VMEM(packed, jnp.float32),
            dma((2 * CHUNKS + 3,)), dma((CHUNKS,)), dma((CHUNKS,)), dma((4 * CHUNKS,)), dma((4 * CHUNKS,)),
            dma((1,)), dma((1,)), dma((4,)), dma((4,)),
            dma((2 * n_plane * CHUNKS,)), dma((2 * n_plane * CHUNKS,)),
            dma((2 * CHUNKS,)), dma((2 * CHUNKS,)),
            dma((n_chips,)), dma((n_chips,)), dma((1,)), dma((1,)),
            pltpu.SemaphoreType.REGULAR((1,)),
        ],
        compiler_params=pltpu.CompilerParams(
            collective_id=0, has_side_effects=True, vmem_limit_bytes=64 * 1024 * 1024 - 400 * 1024
        ),
    )(defect_level, psi, base_potential, defect_site)
    return pl.pallas_call(
        store,
        out_shape=(
            jax.ShapeDtypeStruct(filtered.shape, filtered.dtype),
            jax.ShapeDtypeStruct(correlation.shape, correlation.dtype),
        ),
        in_specs=[vmem, vmem],
        out_specs=(hbm, hbm),
        scratch_shapes=[dma((2,))],
    )(*(pltpu.with_memory_space_constraint(a, pltpu.VMEM) for a in (filtered, correlation)))


def solution(mesh):
    in_specs = (P("band", "dx", "dy", None), P("dx", "dy", None), P("dx", "dy", None), P())
    out_specs = (P("band", "dx", "dy", None), P("band", "dy"))
    n_band, n_dx, n_dy = mesh.shape["band"], mesh.shape["dx"], mesh.shape["dy"]

    def body(psi, base_potential, defect_site, defect_level):
        nb, nx, ny, nz = psi.shape
        fits = (
            n_dx == 2 and nx == 2 and nz == 128 and nb == 64
            and n_dy == 4 and n_band == 4 and ny == 8
        )
        run = fused if fits else shards
        return run(psi, base_potential, defect_site, defect_level)

    return jax.shard_map(body, mesh=mesh, in_specs=in_specs, out_specs=out_specs, check_vma=False)
```

```python
import functools

import jax
import jax.numpy as jnp
from jax import lax
from jax.experimental import pallas as pl
from jax.experimental.pallas import tpu as pltpu
from jax.sharding import PartitionSpec as P

SELF_WEIGHT = -2.5
NEAR_WEIGHT = 4.0 / 3.0
FAR_WEIGHT = -1.0 / 12.0
FILTER_CENTER = 5.5
FILTER_HALF = 3.5


def with_halo(block, sides, width):
    for axis, dim in sides:
        count = lax.axis_size(axis)
        forward = [(i, i + 1) for i in range(count - 1)]
        forward.append((count - 1, 0))
        backward = [(target, source) for source, target in forward]
        low = lax.ppermute(
            lax.slice_in_dim(block, block.shape[dim] - width, None, axis=dim), axis, forward
        )
        high = lax.ppermute(lax.slice_in_dim(block, 0, width, axis=dim), axis, backward)
        block = jnp.concatenate([low, block, high], axis=dim)
    return block


def hamiltonian(field, potential):
    padded = with_halo(field, (("dx", 1), ("dy", 2)), 2).astype(jnp.float32)
    width_x = field.shape[1]
    width_y = field.shape[2]
    center = padded[:, 2 : 2 + width_x, 2 : 2 + width_y, :]
    laplace = 3.0 * SELF_WEIGHT * center
    laplace = laplace + NEAR_WEIGHT * (
        padded[:, 3 : 3 + width_x, 2 : 2 + width_y, :]
        + padded[:, 1 : 1 + width_x, 2 : 2 + width_y, :]
    )
    laplace = laplace + FAR_WEIGHT * (
        padded[:, 4 : 4 + width_x, 2 : 2 + width_y, :] + padded[:, 0:width_x, 2 : 2 + width_y, :]
    )
    laplace = laplace + NEAR_WEIGHT * (
        padded[:, 2 : 2 + width_x, 3 : 3 + width_y, :]
        + padded[:, 2 : 2 + width_x, 1 : 1 + width_y, :]
    )
    laplace = laplace + FAR_WEIGHT * (
        padded[:, 2 : 2 + width_x, 4 : 4 + width_y, :] + padded[:, 2 : 2 + width_x, 0:width_y, :]
    )
    laplace = laplace + NEAR_WEIGHT * (jnp.roll(center, 1, 3) + jnp.roll(center, -1, 3))
    laplace = laplace + FAR_WEIGHT * (jnp.roll(center, 2, 3) + jnp.roll(center, -2, 3))
    return (-0.5 * laplace + potential[None] * center, center)


def shards(psi, base_potential, defect_site, defect_level):
    levels = jnp.arange(defect_level.shape[0], dtype=jnp.int32)
    picked = jnp.sum(
        jnp.where(
            defect_site[None] == levels[:, None, None, None],
            defect_level[:, None, None, None],
            jnp.float32(0.0),
        ),
        axis=0,
    )
    potential = base_potential + picked
    applied, start_field = hamiltonian(psi, potential)
    first = ((applied - FILTER_CENTER * start_field) / FILTER_HALF).astype(jnp.bfloat16)
    applied_next, first_wide = hamiltonian(first, potential)
    filtered = (
        2.0 * (applied_next - FILTER_CENTER * first_wide) / FILTER_HALF - start_field
    ).astype(jnp.bfloat16)
    nb_dev = psi.shape[0]
    cells_all = (
        psi.shape[1] * psi.shape[2] * psi.shape[3] * lax.axis_size("dx") * lax.axis_size("dy")
    )
    flat = filtered.reshape(nb_dev, -1)
    tile = lax.dot_general(
        flat,
        lax.all_gather(flat, "band", axis=0, tiled=True),
        (((1,), (1,)), ((), ())),
        preferred_element_type=jnp.float32,
    )
    column_part = lax.psum_scatter(
        tile.astype(jnp.bfloat16), "dy", scatter_dimension=1, tiled=True
    ).astype(jnp.float32)
    columns = lax.psum(column_part, "dx")
    correlation = columns / cells_all
    return (filtered, correlation)


MESH = pl.DeviceIdType.MESH
CHUNKS = 2


def apply_filter(load, x, j, coef):
    center = load(x, j)
    near = load((x + 1) % 4, j) + load((x + 3) % 4, j)
    far_x = load((x + 2) % 4, j)
    far = far_x + far_x
    near = near + load(x, j + 1) + load(x, j - 1)
    far = far + load(x, j + 2) + load(x, j - 2)
    near = near + pltpu.roll(center, 1, 1) + pltpu.roll(center, 127, 1)
    far = far + pltpu.roll(center, 2, 1) + pltpu.roll(center, 126, 1)
    rows = center.shape[0]
    scaled = (center.reshape(rows // 8, 8, 128) * coef[None]).reshape(rows, 128)
    return (
        scaled
        + near * (-0.5 * NEAR_WEIGHT / FILTER_HALF)
        + far * (-0.5 * FAR_WEIGHT / FILTER_HALF)
    )


def over(low, count, body, part):
    group = next(size for size in (8, 4, 2, 1) if count % size == 0)

    def step(i, carry):
        for k in range(group):
            body(part, low + i * group + k)
        return carry

    lax.fori_loop(0, count // group, step, 0)


def kernel(
    n_band, n_dy, cells_all,
    level_hbm, psi_hbm, base_hbm, site_hbm,
    out_ref, corr_ref,
    level_ref, psi_ref, base_ref, site_ref, weight, weight_in, edge, edge_in,
    psi_t, coef, halo, wide, first, done, out_t, gather, block, own_block, sums, pair_out, pair_in,
    load_sem, pair_psi_send, pair_psi_recv, psi_send, psi_recv, weight_send, weight_recv,
    edge_send, edge_recv, gather_send, gather_recv, out_send, out_recv, sum_send, sum_recv,
    pair_send, pair_recv, greeted,
):
    band, core, dy = lax.axis_index("band"), lax.axis_index("dx"), lax.axis_index("dy")
    nb = psi_ref.shape[0]
    half = nb // 2
    chunk = half // CHUNKS
    ny = psi_ref.shape[2]
    other = 1 - core
    side_a = (dy < n_dy // 2).astype(jnp.int32)
    side_b = 1 - side_a
    inner = dy + 2 * side_a - 1
    outer = lax.rem(dy - 2 * side_a + 1 + n_dy, n_dy)

    barrier = pltpu.get_barrier_semaphore()

    def signal(semaphore, device):
        pl.semaphore_signal(semaphore, inc=1, device_id=device, device_id_type=MESH)

    pieces = [pl.ds(h * half + g * chunk, chunk) for g in range(CHUNKS) for h in range(2)]
    loads = [
        pltpu.make_async_copy(src, dst, load_sem.at[index])
        for index, (src, dst) in enumerate(
            [(psi_hbm.at[rows], psi_ref.at[rows]) for rows in pieces]
            + [(level_hbm, level_ref), (site_hbm, site_ref), (base_hbm, base_ref)]
        )
    ]
    for load in loads:
        load.start()
    last = dy == n_dy - 1
    for h in range(2):
        signal(barrier, (band, h, inner))
    signal(barrier, (band, other, dy))

    @pl.when(jnp.logical_not(last))
    def _():
        for h in range(2):
            signal(barrier, (band, h, outer))

    @pl.when(dy < n_dy - 2)
    def _():
        for i in range(1, n_band):
            for h in range(2):
                signal(barrier, (lax.rem(band + i, n_band), h, dy))

    @pl.when(last)
    def _():
        pl.semaphore_wait(barrier, 5)
        signal(greeted.at[0], (band, core, 0))

    for load in loads[2 * CHUNKS :]:
        load.wait()

    site = site_ref[...]
    picked = jnp.zeros(site.shape, jnp.float32)
    for level in range(level_ref.shape[0]):
        picked = picked + jnp.where(site == level, level_ref[level], jnp.float32(0.0))
    weight[...] = (
        base_ref[...] + picked - (1.5 * SELF_WEIGHT + FILTER_CENTER)
    ) * (1.0 / FILTER_HALF)
    for x in range(2):
        edge[0, 2 * x : 2 * x + 2] = weight[x, ny - 2 : ny]
        edge[1, 2 * x : 2 * x + 2] = weight[x, 0:2]

    def turn(g):
        for h in range(2):
            loads[2 * g + h].wait()
            rows = pieces[2 * g + h]
            for x in range(2):
                psi_t[x, :, rows] = jnp.transpose(
                    psi_ref[rows, x].astype(jnp.float32), (1, 0, 2)
                ).astype(jnp.bfloat16)

    turn(0)

    @pl.when(dy == 0)
    def _():
        pl.semaphore_wait(barrier, 2 * n_band + 1)

    @pl.when(dy == 1)
    def _():
        pl.semaphore_wait(barrier, 2 * n_band + 3)

    @pl.when(dy == n_dy - 2)
    def _():
        pl.semaphore_wait(barrier, 5)


    layers = pl.ds(2 * core, 2)

    def copy_of(src, dst, send_sem, recv_sem, device):
        return pltpu.make_async_remote_copy(
            src_ref=src, dst_ref=dst, send_sem=send_sem, recv_sem=recv_sem,
            device_id=device, device_id_type=MESH,
        )

    def send(*args):
        copy = copy_of(*args)
        copy.start()
        return copy

    def bands(where, g):
        return pl.ds(pl.multiple_of(where * half + g * chunk, chunk), chunk)

    def part_of(g):
        return pl.ds(g * chunk, chunk)

    def halo_copy(side, target, g, h):
        slot = (side * CHUNKS + g) * 2
        return copy_of(
            psi_t.at[:, pl.ds((1 - side) * (ny - 4), 4), bands(h, g)],
            halo.at[layers, pl.ds(side * (ny + 4), 4), part_of(g)],
            psi_send.at[slot + h], psi_recv.at[slot + core], (band, h, target),
        )

    def edge_copy(side, target, h):
        return copy_of(
            edge.at[side], edge_in.at[side, core],
            edge_send.at[2 * side + h], edge_recv.at[2 * side + core], (band, h, target),
        )

    def send_part(g, side, target):
        for h in range(2):
            if g == 0:
                edge_copy(side, target, h).start()
            halo_copy(side, target, g, h).start()

    def send_side(side, target):
        for g in range(CHUNKS):
            send_part(g, side, target)

    @pl.when(dy > 0)
    def _():
        send_part(0, side_b, inner)
        send_part(0, side_a, outer)

    turn(1)

    @pl.when(dy > 0)
    def _():
        send_part(1, side_b, inner)
        send_part(1, side_a, outer)

    pairs = [
        send(
            psi_t.at[:, :, bands(other, g)], halo.at[layers, pl.ds(4, ny), part_of(g)],
            pair_psi_send.at[g], pair_psi_recv.at[g], (band, other, dy),
        )
        for g in range(CHUNKS)
    ]
    potential = send(
        weight, weight_in, weight_send.at[0], weight_recv.at[0], (band, other, dy)
    )

    @pl.when(dy == 0)
    def _():
        send_side(side_b, inner)
        pl.semaphore_wait(greeted.at[0], 1)
        send_side(side_a, outer)

    @pl.when(dy == n_dy - 2)
    def _():
        pl.semaphore_wait(greeted.at[1], 1)

    @pl.when(jnp.logical_and(dy > 0, jnp.logical_not(last)))
    def _():
        for i in range(1, n_band):
            signal(greeted.at[0], (lax.rem(band + i, n_band), core, dy))
        pl.semaphore_wait(greeted.at[0], n_band - 1)
        signal(greeted.at[1], (band, core, dy + 1))

    own = pl.ds(pl.multiple_of(core * half, half), half)
    for x in range(2):
        for y in range(ny):
            coef[2 * core + x, 2 + y] = jnp.broadcast_to(weight[x, y : y + 1], (8, 128))
            wide[2 * core + x, 4 + y] = psi_t[x, y, own].astype(jnp.float32)

    potential.wait()
    for x in range(2):
        for y in range(ny):
            coef[2 * other + x, 2 + y] = jnp.broadcast_to(weight_in[x, y : y + 1], (8, 128))

    def step_one(part, j):
        for x in range(4):
            value = apply_filter(lambda a, r: wide[a, r, part], x, j + 2, coef[x, j])
            first[x, j, part] = value.astype(jnp.bfloat16).astype(jnp.float32)

    def step_two(part, y):
        for x in range(4):
            value = apply_filter(lambda a, r: first[a, r, part], x, y + 2, coef[x, y + 2])
            done[x, y, part] = (2.0 * value - wide[x, y + 4, part]).astype(jnp.bfloat16)

    def widen(part, j):
        for x in range(4):
            wide[x, j, part] = halo[x, j, part].astype(jnp.float32)

    for g in range(CHUNKS):
        part = part_of(g)
        pairs[g].wait()
        for x in range(2):
            for y in range(ny):
                wide[2 * other + x, 4 + y, part] = halo[2 * other + x, 4 + y, part].astype(jnp.float32)
        over(4, ny - 4, step_one, part)

    me = 2 * band + core
    def row_of(side, i):
        return side * (ny // 2) + i

    def out_copy(stage, g):
        rows = pl.ds(sides[stage] * (ny // 2), ny // 2)
        place = pl.ds(pl.multiple_of(core * half + g * chunk, chunk), chunk)
        return copy_of(
            done.at[pl.ds(2 * other, 2), rows, part_of(g)], out_t.at[:, rows, place],
            out_send.at[stage * CHUNKS + g], out_recv.at[stage * CHUNKS + g], (band, other, dy),
        )

    def gather_copy(stage, g, i, h):
        place = pl.ds(pl.multiple_of(band * nb + core * half + g * chunk, chunk), chunk)
        slot = stage * CHUNKS + g
        return copy_of(
            done.at[pl.ds(2 * h, 2), row_of(sides[stage], i), part_of(g)],
            gather.at[:, stage, place],
            gather_send.at[(i * 2 + h) * 2 * CHUNKS + slot], gather_recv.at[me * 2 * CHUNKS + slot],
            (i, h, dy),
        )

    sides = (side_a, side_b)

    @pl.when(last)
    def _():
        pl.semaphore_wait(greeted.at[1], 1)

    for stage, side in enumerate(sides):
        for g in range(CHUNKS):
            part = part_of(g)
            if g == 0:
                for h in range(2):
                    copy_of(
                        edge.at[side], edge_in.at[side, h],
                        edge_send.at[2 * side + h], edge_recv.at[2 * side + h], (band, h, inner),
                    ).wait_recv()
                for source in range(2):
                    for x in range(2):
                        for y in range(2):
                            coef[2 * source + x, side * (ny + 2) + y] = jnp.broadcast_to(
                                edge_in[side, source, 2 * x + y : 2 * x + y + 1], (8, 128)
                            )
            for h in range(2):
                slot = (side * CHUNKS + g) * 2 + h
                copy_of(
                    psi_t.at[:, pl.ds(0, 4), bands(h, g)],
                    halo.at[pl.ds(2 * h, 2), pl.ds(side * (ny + 4), 4), part],
                    psi_send.at[slot], psi_recv.at[slot], (band, h, inner),
                ).wait_recv()
            over(side * (ny + 4), 4, widen, part)
            over(side * ny, 4, step_one, part)
            over(side * (ny // 2), ny // 2, step_two, part)
            for i in range(n_band):
                for h in range(2):

                    @pl.when(me != 2 * i + h)
                    def _():
                        gather_copy(stage, g, i, h).start()

            out_copy(stage, g).start()

    for g in range(CHUNKS):
        place = pl.ds(pl.multiple_of(band * nb + core * half + g * chunk, chunk), chunk)
        for x in range(2):
            for stage in range(2):
                gather[x, stage, place] = done[2 * core + x, row_of(sides[stage], band), part_of(g)]
    for x in range(2):
        for y in range(ny):
            out_t[x, y, own] = done[2 * core + x, y]
    for stage in range(2):
        for g in range(CHUNKS):
            out_copy(stage, g).wait()

    def pack(tile):
        top, bottom = tile[:half], tile[half:]
        return (
            jnp.where(low, top, pltpu.roll(bottom, 64, 1)).astype(jnp.bfloat16),
            jnp.where(low, pltpu.roll(top, 64, 1), bottom).astype(jnp.bfloat16),
        )

    low = lax.broadcasted_iota(jnp.int32, (half, 128), 1) < 64
    cells = jnp.concatenate([out_t[x, y] for x in range(2) for y in range(ny)], axis=1)
    square = lax.dot_general(
        cells, cells, (((1,), (1,)), ((), ())), preferred_element_type=jnp.float32
    )
    square = jnp.concatenate([square, square], axis=1)
    own_block[...] = jnp.where(low, square[:half], square[half:]).astype(jnp.bfloat16)

    def own_copy(slot):
        return copy_of(
            own_block, sums.at[slot * n_band + band],
            sum_send.at[band * n_band + band], sum_recv.at[slot * n_band + band],
            (band, core, band),
        )

    @pl.when(dy != band)
    def _():
        own_copy(dy).start()

    for j in range(1, 2 * n_band):
        source = lax.rem(me + j, 2 * n_band)
        for g in range(CHUNKS):
            place = pl.ds(pl.multiple_of(source * half + g * chunk, chunk), chunk)
            for stage in range(2):
                slot = source * 2 * CHUNKS + stage * CHUNKS + g
                copy_of(
                    gather.at[:, stage, place], gather.at[:, stage, place],
                    gather_send.at[slot], gather_recv.at[slot],
                    (lax.div(source, 2), lax.rem(source, 2), dy),
                ).wait_recv()

    total = None
    for x in range(2):
        cells = jnp.concatenate([gather[x, y] for y in range(2)], axis=1)
        term = lax.dot_general(
            cells, cells, (((1,), (1,)), ((), ())), preferred_element_type=jnp.float32
        )
        total = term if total is None else total + term
    for i in range(n_band):
        for k in range(n_dy // 2):
            tile = total[nb * i : nb * i + nb, 128 * k : 128 * k + 128]
            block[i, 2 * k], block[i, 2 * k + 1] = pack(tile)
    here = dy * n_band + band
    n_chips = n_band * n_dy

    def sum_copy(to_band, to_dy):
        return copy_of(
            block.at[to_band, to_dy], sums.at[here], sum_send.at[to_dy * n_band + to_band],
            sum_recv.at[here], (to_band, core, to_dy),
        )

    low_half = (dy < n_dy // 2).astype(jnp.int32)
    targets = [
        (i, low_half * (n_dy - 1 - k) + (1 - low_half) * k) for k in range(n_dy) for i in range(n_band)
    ]

    def each_target(act):
        for to_band, to_dy in targets:
            itself = jnp.logical_and(to_band == band, to_dy == dy)

            @pl.when(jnp.logical_not(jnp.logical_or(itself, to_dy == to_band)))
            def _():
                act(sum_copy(to_band, to_dy))

    each_target(lambda copy: copy.start())

    for x in range(2):
        out_ref[:, x] = jnp.transpose(out_t[x].astype(jnp.float32), (1, 0, 2)).astype(jnp.bfloat16)
    for side in range(2):
        for h in range(2):
            edge_copy(side, inner, h).wait_send()
            for g in range(CHUNKS):
                halo_copy(side, inner, g, h).wait_send()
    for i in range(n_band):
        for h in range(2):

            @pl.when(me != 2 * i + h)
            def _():
                for stage in range(2):
                    for g in range(CHUNKS):
                        gather_copy(stage, g, i, h).wait_send()

    def landed(slot):
        copy_of(
            own_block, sums.at[slot], sum_send.at[slot], sum_recv.at[slot], (band, other, dy)
        ).wait_recv()

    @pl.when(dy == band)
    def _():
        result = own_block[...].astype(jnp.float32)
        for j in range(1, n_dy):
            slot = lax.rem(dy + j, n_dy) * n_band + band
            landed(slot)
            result = result + sums[slot].astype(jnp.float32)
        pair_out[...] = result

    @pl.when(dy != band)
    def _():
        own_copy(dy).wait_send()
        result = block[band, dy].astype(jnp.float32)
        for j in range(1, n_chips):
            slot = lax.rem(here + j, n_chips)
            landed(slot)
            result = result + sums[slot].astype(jnp.float32)
        pair_out[...] = result

    result = pair_out[...]
    copy = send(pair_out, pair_in, pair_send.at[0], pair_recv.at[0], (band, other, dy))
    copy.wait()
    each_target(lambda copy: copy.wait_send())

    result = (result + pair_in[...]) * (1.0 / cells_all)
    corr_ref[pl.ds(0, half), :] = result[:, :64]
    corr_ref[pl.ds(half, half), :] = pltpu.roll(result, 64, 1)[:, :64]


def store(filtered, correlation, filtered_hbm, correlation_hbm, sem):
    pairs = ((correlation, correlation_hbm), (filtered, filtered_hbm))
    copies = [pltpu.make_async_copy(a, b, sem.at[i]) for i, (a, b) in enumerate(pairs)]
    for copy in copies:
        copy.start()
    for copy in copies:
        copy.wait()


def fused(psi, base_potential, defect_site, defect_level):
    nb, nx, ny, nz = psi.shape
    n_band, n_dy = lax.axis_size("band"), lax.axis_size("dy")
    half, per = nb // 2, ny // n_band
    cells_all = nx * ny * nz * 2 * n_dy
    dma = pltpu.SemaphoreType.DMA
    n_plane, n_chips = 2 * n_band, n_band * n_dy
    vmem = pl.BlockSpec(memory_space=pltpu.VMEM)
    hbm = pl.BlockSpec(memory_space=pltpu.HBM)
    packed = (half, 128)
    filtered, correlation = pl.pallas_call(
        functools.partial(kernel, n_band, n_dy, cells_all),
        out_shape=(
            pltpu.VMEM(psi.shape, jnp.bfloat16),
            pltpu.VMEM((nb, nb * n_band // n_dy), jnp.float32),
        ),
        in_specs=[hbm, hbm, hbm, hbm],
        out_specs=(vmem, vmem),
        scratch_shapes=[
            pltpu.SMEM(defect_level.shape, jnp.float32),
            pltpu.VMEM(psi.shape, jnp.bfloat16),
            pltpu.VMEM(base_potential.shape, jnp.float32),
            pltpu.VMEM(defect_site.shape, jnp.int32),
            pltpu.VMEM(base_potential.shape, jnp.float32),
            pltpu.VMEM(base_potential.shape, jnp.float32),
            pltpu.VMEM((2, 4, nz), jnp.float32),
            pltpu.VMEM((2, 2, 4, nz), jnp.float32),
            pltpu.VMEM((nx, ny, nb, nz), jnp.bfloat16),
            pltpu.VMEM((2 * nx, ny + 4, 8, nz), jnp.float32),
            pltpu.VMEM((2 * nx, ny + 8, half, nz), jnp.bfloat16),
            pltpu.VMEM((2 * nx, ny + 8, half, nz), jnp.float32),
            pltpu.VMEM((2 * nx, ny + 4, half, nz), jnp.float32),
            pltpu.VMEM((2 * nx, ny, half, nz), jnp.bfloat16),
            pltpu.VMEM((nx, ny, nb, nz), jnp.bfloat16),
            pltpu.VMEM((nx, per, nb * n_band, nz), jnp.bfloat16),
            pltpu.VMEM((n_band, n_dy) + packed, jnp.bfloat16),
            pltpu.VMEM(packed, jnp.bfloat16),
            pltpu.VMEM((n_chips,) + packed, jnp.bfloat16),
            pltpu.VMEM(packed, jnp.float32),
            pltpu.VMEM(packed, jnp.float32),
            dma((2 * CHUNKS + 3,)), dma((CHUNKS,)), dma((CHUNKS,)), dma((4 * CHUNKS,)), dma((4 * CHUNKS,)),
            dma((1,)), dma((1,)), dma((4,)), dma((4,)),
            dma((2 * n_plane * CHUNKS,)), dma((2 * n_plane * CHUNKS,)),
            dma((2 * CHUNKS,)), dma((2 * CHUNKS,)),
            dma((n_chips,)), dma((n_chips,)), dma((1,)), dma((1,)),
            pltpu.SemaphoreType.REGULAR((2,)),
        ],
        compiler_params=pltpu.CompilerParams(
            collective_id=0, has_side_effects=True, vmem_limit_bytes=64 * 1024 * 1024 - 400 * 1024
        ),
    )(defect_level, psi, base_potential, defect_site)
    return pl.pallas_call(
        store,
        out_shape=(
            jax.ShapeDtypeStruct(filtered.shape, filtered.dtype),
            jax.ShapeDtypeStruct(correlation.shape, correlation.dtype),
        ),
        in_specs=[vmem, vmem],
        out_specs=(hbm, hbm),
        scratch_shapes=[dma((2,))],
    )(*(pltpu.with_memory_space_constraint(a, pltpu.VMEM) for a in (filtered, correlation)))


def solution(mesh):
    in_specs = (P("band", "dx", "dy", None), P("dx", "dy", None), P("dx", "dy", None), P())
    out_specs = (P("band", "dx", "dy", None), P("band", "dy"))
    n_band, n_dx, n_dy = mesh.shape["band"], mesh.shape["dx"], mesh.shape["dy"]

    def body(psi, base_potential, defect_site, defect_level):
        nb, nx, ny, nz = psi.shape
        fits = (
            n_dx == 2 and nx == 2 and nz == 128 and nb == 64
            and n_dy == 4 and n_band == 4 and ny == 8
        )
        run = fused if fits else shards
        return run(psi, base_potential, defect_site, defect_level)

    return jax.shard_map(body, mesh=mesh, in_specs=in_specs, out_specs=out_specs, check_vma=False)
```

```python
import functools

import jax
import jax.numpy as jnp
from jax import lax
from jax.experimental import pallas as pl
from jax.experimental.pallas import tpu as pltpu
from jax.sharding import PartitionSpec as P

SELF_WEIGHT = -2.5
NEAR_WEIGHT = 4.0 / 3.0
FAR_WEIGHT = -1.0 / 12.0
FILTER_CENTER = 5.5
FILTER_HALF = 3.5


def with_halo(block, sides, width):
    for axis, dim in sides:
        count = lax.axis_size(axis)
        forward = [(i, i + 1) for i in range(count - 1)]
        forward.append((count - 1, 0))
        backward = [(target, source) for source, target in forward]
        low = lax.ppermute(
            lax.slice_in_dim(block, block.shape[dim] - width, None, axis=dim), axis, forward
        )
        high = lax.ppermute(lax.slice_in_dim(block, 0, width, axis=dim), axis, backward)
        block = jnp.concatenate([low, block, high], axis=dim)
    return block


def hamiltonian(field, potential):
    padded = with_halo(field, (("dx", 1), ("dy", 2)), 2).astype(jnp.float32)
    width_x = field.shape[1]
    width_y = field.shape[2]
    center = padded[:, 2 : 2 + width_x, 2 : 2 + width_y, :]
    laplace = 3.0 * SELF_WEIGHT * center
    laplace = laplace + NEAR_WEIGHT * (
        padded[:, 3 : 3 + width_x, 2 : 2 + width_y, :]
        + padded[:, 1 : 1 + width_x, 2 : 2 + width_y, :]
    )
    laplace = laplace + FAR_WEIGHT * (
        padded[:, 4 : 4 + width_x, 2 : 2 + width_y, :] + padded[:, 0:width_x, 2 : 2 + width_y, :]
    )
    laplace = laplace + NEAR_WEIGHT * (
        padded[:, 2 : 2 + width_x, 3 : 3 + width_y, :]
        + padded[:, 2 : 2 + width_x, 1 : 1 + width_y, :]
    )
    laplace = laplace + FAR_WEIGHT * (
        padded[:, 2 : 2 + width_x, 4 : 4 + width_y, :] + padded[:, 2 : 2 + width_x, 0:width_y, :]
    )
    laplace = laplace + NEAR_WEIGHT * (jnp.roll(center, 1, 3) + jnp.roll(center, -1, 3))
    laplace = laplace + FAR_WEIGHT * (jnp.roll(center, 2, 3) + jnp.roll(center, -2, 3))
    return (-0.5 * laplace + potential[None] * center, center)


def shards(psi, base_potential, defect_site, defect_level):
    levels = jnp.arange(defect_level.shape[0], dtype=jnp.int32)
    picked = jnp.sum(
        jnp.where(
            defect_site[None] == levels[:, None, None, None],
            defect_level[:, None, None, None],
            jnp.float32(0.0),
        ),
        axis=0,
    )
    potential = base_potential + picked
    applied, start_field = hamiltonian(psi, potential)
    first = ((applied - FILTER_CENTER * start_field) / FILTER_HALF).astype(jnp.bfloat16)
    applied_next, first_wide = hamiltonian(first, potential)
    filtered = (
        2.0 * (applied_next - FILTER_CENTER * first_wide) / FILTER_HALF - start_field
    ).astype(jnp.bfloat16)
    nb_dev = psi.shape[0]
    cells_all = (
        psi.shape[1] * psi.shape[2] * psi.shape[3] * lax.axis_size("dx") * lax.axis_size("dy")
    )
    flat = filtered.reshape(nb_dev, -1)
    tile = lax.dot_general(
        flat,
        lax.all_gather(flat, "band", axis=0, tiled=True),
        (((1,), (1,)), ((), ())),
        preferred_element_type=jnp.float32,
    )
    column_part = lax.psum_scatter(
        tile.astype(jnp.bfloat16), "dy", scatter_dimension=1, tiled=True
    ).astype(jnp.float32)
    columns = lax.psum(column_part, "dx")
    correlation = columns / cells_all
    return (filtered, correlation)


MESH = pl.DeviceIdType.MESH
CHUNKS = 2


def apply_filter(load, x, j, coef):
    center = load(x, j)
    near = load((x + 1) % 4, j) + load((x + 3) % 4, j)
    far_x = load((x + 2) % 4, j)
    far = far_x + far_x
    near = near + load(x, j + 1) + load(x, j - 1)
    far = far + load(x, j + 2) + load(x, j - 2)
    near = near + pltpu.roll(center, 1, 1) + pltpu.roll(center, 127, 1)
    far = far + pltpu.roll(center, 2, 1) + pltpu.roll(center, 126, 1)
    rows = center.shape[0]
    scaled = (center.reshape(rows // 8, 8, 128) * coef[None]).reshape(rows, 128)
    return (
        scaled
        + near * (-0.5 * NEAR_WEIGHT / FILTER_HALF)
        + far * (-0.5 * FAR_WEIGHT / FILTER_HALF)
    )


def over(low, count, body, part):
    group = next(size for size in (8, 4, 2, 1) if count % size == 0)

    def step(i, carry):
        for k in range(group):
            body(part, low + i * group + k)
        return carry

    lax.fori_loop(0, count // group, step, 0)


def kernel(
    n_band, n_dy, cells_all,
    level_hbm, psi_hbm, base_hbm, site_hbm,
    out_ref, corr_ref,
    level_ref, psi_ref, base_ref, site_ref, weight, weight_in, edge, edge_in,
    psi_t, coef, halo, wide, first, done, out_t, gather, block, own_block, sums, pair_out, pair_in,
    load_sem, pair_psi_send, pair_psi_recv, psi_send, psi_recv, weight_send, weight_recv,
    edge_send, edge_recv, gather_send, gather_recv, out_send, out_recv, sum_send, sum_recv,
    pair_send, pair_recv, greeted,
):
    band, core, dy = lax.axis_index("band"), lax.axis_index("dx"), lax.axis_index("dy")
    nb = psi_ref.shape[0]
    half = nb // 2
    chunk = half // CHUNKS
    ny = psi_ref.shape[2]
    other = 1 - core
    side_a = (dy < n_dy // 2).astype(jnp.int32)
    side_b = 1 - side_a
    inner = dy + 2 * side_a - 1
    outer = lax.rem(dy - 2 * side_a + 1 + n_dy, n_dy)

    barrier = pltpu.get_barrier_semaphore()

    def signal(semaphore, device):
        pl.semaphore_signal(semaphore, inc=1, device_id=device, device_id_type=MESH)

    pieces = [pl.ds(h * half + g * chunk, chunk) for g in range(CHUNKS) for h in range(2)]
    loads = [
        pltpu.make_async_copy(src, dst, load_sem.at[index])
        for index, (src, dst) in enumerate(
            [(psi_hbm.at[rows], psi_ref.at[rows]) for rows in pieces]
            + [(level_hbm, level_ref), (site_hbm, site_ref), (base_hbm, base_ref)]
        )
    ]
    for load in loads:
        load.start()
    last = dy == n_dy - 1
    for h in range(2):
        signal(barrier, (band, h, inner))
    signal(barrier, (band, other, dy))

    @pl.when(jnp.logical_not(last))
    def _():
        for h in range(2):
            signal(barrier, (band, h, outer))

    @pl.when(dy < n_dy - 2)
    def _():
        for i in range(1, n_band):
            for h in range(2):
                signal(barrier, (lax.rem(band + i, n_band), h, dy))

    @pl.when(last)
    def _():
        pl.semaphore_wait(barrier, 5)
        signal(greeted.at[0], (band, core, 0))

    for load in loads[2 * CHUNKS :]:
        load.wait()

    site = site_ref[...]
    picked = jnp.zeros(site.shape, jnp.float32)
    for level in range(level_ref.shape[0]):
        picked = picked + jnp.where(site == level, level_ref[level], jnp.float32(0.0))
    weight[...] = (
        base_ref[...] + picked - (1.5 * SELF_WEIGHT + FILTER_CENTER)
    ) * (1.0 / FILTER_HALF)
    for x in range(2):
        edge[0, 2 * x : 2 * x + 2] = weight[x, ny - 2 : ny]
        edge[1, 2 * x : 2 * x + 2] = weight[x, 0:2]

    def turn(g):
        for h in range(2):
            loads[2 * g + h].wait()
            rows = pieces[2 * g + h]
            for x in range(2):
                psi_t[x, :, rows] = jnp.transpose(
                    psi_ref[rows, x].astype(jnp.float32), (1, 0, 2)
                ).astype(jnp.bfloat16)

    turn(0)

    @pl.when(dy == 0)
    def _():
        pl.semaphore_wait(barrier, 2 * n_band + 1)

    @pl.when(dy == 1)
    def _():
        pl.semaphore_wait(barrier, 2 * n_band + 3)

    @pl.when(dy == n_dy - 2)
    def _():
        pl.semaphore_wait(barrier, 5)


    layers = pl.ds(2 * core, 2)

    def copy_of(src, dst, send_sem, recv_sem, device):
        return pltpu.make_async_remote_copy(
            src_ref=src, dst_ref=dst, send_sem=send_sem, recv_sem=recv_sem,
            device_id=device, device_id_type=MESH,
        )

    def send(*args):
        copy = copy_of(*args)
        copy.start()
        return copy

    def bands(where, g):
        return pl.ds(pl.multiple_of(where * half + g * chunk, chunk), chunk)

    def part_of(g):
        return pl.ds(g * chunk, chunk)

    def halo_copy(side, target, g, h):
        slot = (side * CHUNKS + g) * 2
        return copy_of(
            psi_t.at[:, pl.ds((1 - side) * (ny - 4), 4), bands(h, g)],
            halo.at[layers, pl.ds(side * (ny + 4), 4), part_of(g)],
            psi_send.at[slot + h], psi_recv.at[slot + core], (band, h, target),
        )

    def edge_copy(side, target, h):
        return copy_of(
            edge.at[side], edge_in.at[side, core],
            edge_send.at[2 * side + h], edge_recv.at[2 * side + core], (band, h, target),
        )

    def send_part(g, side, target):
        for h in range(2):
            if g == 0:
                edge_copy(side, target, h).start()
            halo_copy(side, target, g, h).start()

    def send_side(side, target):
        for g in range(CHUNKS):
            send_part(g, side, target)

    @pl.when(dy > 0)
    def _():
        send_part(0, side_b, inner)
        send_part(0, side_a, outer)

    turn(1)

    @pl.when(dy > 0)
    def _():
        send_part(1, side_b, inner)
        send_part(1, side_a, outer)

    pairs = [
        send(
            psi_t.at[:, :, bands(other, g)], halo.at[layers, pl.ds(4, ny), part_of(g)],
            pair_psi_send.at[g], pair_psi_recv.at[g], (band, other, dy),
        )
        for g in range(CHUNKS)
    ]
    potential = send(
        weight, weight_in, weight_send.at[0], weight_recv.at[0], (band, other, dy)
    )

    @pl.when(dy == 0)
    def _():
        send_side(side_b, inner)
        pl.semaphore_wait(greeted.at[0], 1)
        send_side(side_a, outer)

    @pl.when(dy == n_dy - 2)
    def _():
        pl.semaphore_wait(greeted.at[1], 1)

    @pl.when(jnp.logical_and(dy > 0, jnp.logical_not(last)))
    def _():
        for i in range(1, n_band):
            signal(greeted.at[0], (lax.rem(band + i, n_band), core, dy))
        pl.semaphore_wait(greeted.at[0], n_band - 1)
        signal(greeted.at[1], (band, core, dy + 1))

    own = pl.ds(pl.multiple_of(core * half, half), half)
    for x in range(2):
        for y in range(ny):
            coef[2 * core + x, 2 + y] = jnp.broadcast_to(weight[x, y : y + 1], (8, 128))
            wide[2 * core + x, 4 + y] = psi_t[x, y, own].astype(jnp.float32)

    potential.wait()
    for x in range(2):
        for y in range(ny):
            coef[2 * other + x, 2 + y] = jnp.broadcast_to(weight_in[x, y : y + 1], (8, 128))

    def step_one(part, j):
        for x in range(4):
            value = apply_filter(lambda a, r: wide[a, r, part], x, j + 2, coef[x, j])
            first[x, j, part] = value.astype(jnp.bfloat16).astype(jnp.float32)

    def step_two(part, y):
        for x in range(4):
            value = apply_filter(lambda a, r: first[a, r, part], x, y + 2, coef[x, y + 2])
            done[x, y, part] = (2.0 * value - wide[x, y + 4, part]).astype(jnp.bfloat16)

    def widen(part, j):
        for x in range(4):
            wide[x, j, part] = halo[x, j, part].astype(jnp.float32)

    for g in range(CHUNKS):
        part = part_of(g)
        pairs[g].wait()
        for x in range(2):
            for y in range(ny):
                wide[2 * other + x, 4 + y, part] = halo[2 * other + x, 4 + y, part].astype(jnp.float32)
        over(4, ny - 4, step_one, part)

    me = 2 * band + core
    turned = (n_band - 1 - band, lax.rem(band + 2, n_band), band + 1 - 2 * lax.rem(band, 2), band)
    plane = [(i, lax.rem(core + h, 2)) for i in turned[:-1] for h in range(2)] + [(band, other)]
    def row_of(side, i):
        return side * (ny // 2) + i

    def out_copy(stage, g):
        rows = pl.ds(sides[stage] * (ny // 2), ny // 2)
        place = pl.ds(pl.multiple_of(core * half + g * chunk, chunk), chunk)
        return copy_of(
            done.at[pl.ds(2 * other, 2), rows, part_of(g)], out_t.at[:, rows, place],
            out_send.at[stage * CHUNKS + g], out_recv.at[stage * CHUNKS + g], (band, other, dy),
        )

    def gather_copy(stage, g, i, h):
        place = pl.ds(pl.multiple_of(band * nb + core * half + g * chunk, chunk), chunk)
        slot = stage * CHUNKS + g
        return copy_of(
            done.at[pl.ds(2 * h, 2), row_of(sides[stage], i), part_of(g)],
            gather.at[:, stage, place],
            gather_send.at[(i * 2 + h) * 2 * CHUNKS + slot], gather_recv.at[me * 2 * CHUNKS + slot],
            (i, h, dy),
        )

    sides = (side_a, side_b)

    @pl.when(last)
    def _():
        pl.semaphore_wait(greeted.at[1], 1)

    for stage, side in enumerate(sides):
        for g in range(CHUNKS):
            part = part_of(g)
            if g == 0:
                for h in range(2):
                    copy_of(
                        edge.at[side], edge_in.at[side, h],
                        edge_send.at[2 * side + h], edge_recv.at[2 * side + h], (band, h, inner),
                    ).wait_recv()
                for source in range(2):
                    for x in range(2):
                        for y in range(2):
                            coef[2 * source + x, side * (ny + 2) + y] = jnp.broadcast_to(
                                edge_in[side, source, 2 * x + y : 2 * x + y + 1], (8, 128)
                            )
            for h in range(2):
                slot = (side * CHUNKS + g) * 2 + h
                copy_of(
                    psi_t.at[:, pl.ds(0, 4), bands(h, g)],
                    halo.at[pl.ds(2 * h, 2), pl.ds(side * (ny + 4), 4), part],
                    psi_send.at[slot], psi_recv.at[slot], (band, h, inner),
                ).wait_recv()
            over(side * (ny + 4), 4, widen, part)
            over(side * ny, 4, step_one, part)
            over(side * (ny // 2), ny // 2, step_two, part)
            for i, h in plane:
                gather_copy(stage, g, i, h).start()

            out_copy(stage, g).start()

    for g in range(CHUNKS):
        place = pl.ds(pl.multiple_of(band * nb + core * half + g * chunk, chunk), chunk)
        for x in range(2):
            for stage in range(2):
                gather[x, stage, place] = done[2 * core + x, row_of(sides[stage], band), part_of(g)]
    for x in range(2):
        for y in range(ny):
            out_t[x, y, own] = done[2 * core + x, y]
    for stage in range(2):
        for g in range(CHUNKS):
            out_copy(stage, g).wait()

    def pack(tile):
        top, bottom = tile[:half], tile[half:]
        return (
            jnp.where(low, top, pltpu.roll(bottom, 64, 1)).astype(jnp.bfloat16),
            jnp.where(low, pltpu.roll(top, 64, 1), bottom).astype(jnp.bfloat16),
        )

    low = lax.broadcasted_iota(jnp.int32, (half, 128), 1) < 64
    cells = jnp.concatenate([out_t[x, y] for x in range(2) for y in range(ny)], axis=1)
    square = lax.dot_general(
        cells, cells, (((1,), (1,)), ((), ())), preferred_element_type=jnp.float32
    )
    square = jnp.concatenate([square, square], axis=1)
    own_block[...] = jnp.where(low, square[:half], square[half:]).astype(jnp.bfloat16)

    def own_copy(slot):
        return copy_of(
            own_block, sums.at[slot * n_band + band],
            sum_send.at[band * n_band + band], sum_recv.at[slot * n_band + band],
            (band, core, band),
        )

    @pl.when(dy != band)
    def _():
        own_copy(dy).start()

    for j in range(1, 2 * n_band):
        source = lax.rem(me + j, 2 * n_band)
        for g in range(CHUNKS):
            place = pl.ds(pl.multiple_of(source * half + g * chunk, chunk), chunk)
            for stage in range(2):
                slot = source * 2 * CHUNKS + stage * CHUNKS + g
                copy_of(
                    gather.at[:, stage, place], gather.at[:, stage, place],
                    gather_send.at[slot], gather_recv.at[slot],
                    (lax.div(source, 2), lax.rem(source, 2), dy),
                ).wait_recv()

    total = None
    for x in range(2):
        cells = jnp.concatenate([gather[x, y] for y in range(2)], axis=1)
        term = lax.dot_general(
            cells, cells, (((1,), (1,)), ((), ())), preferred_element_type=jnp.float32
        )
        total = term if total is None else total + term
    for i in range(n_band):
        for k in range(n_dy // 2):
            tile = total[nb * i : nb * i + nb, 128 * k : 128 * k + 128]
            block[i, 2 * k], block[i, 2 * k + 1] = pack(tile)
    here = dy * n_band + band
    n_chips = n_band * n_dy

    def sum_copy(to_band, to_dy):
        return copy_of(
            block.at[to_band, to_dy], sums.at[here], sum_send.at[to_dy * n_band + to_band],
            sum_recv.at[here], (to_band, core, to_dy),
        )

    low_half = (dy < n_dy // 2).astype(jnp.int32)
    targets = [
        (i, low_half * (n_dy - 1 - k) + (1 - low_half) * k) for k in range(n_dy) for i in turned
    ]

    def each_target(act):
        for to_band, to_dy in targets:
            itself = jnp.logical_and(to_band == band, to_dy == dy)

            @pl.when(jnp.logical_not(jnp.logical_or(itself, to_dy == to_band)))
            def _():
                act(sum_copy(to_band, to_dy))

    each_target(lambda copy: copy.start())

    for x in range(2):
        out_ref[:, x] = jnp.transpose(out_t[x].astype(jnp.float32), (1, 0, 2)).astype(jnp.bfloat16)
    for side in range(2):
        for h in range(2):
            edge_copy(side, inner, h).wait_send()
            for g in range(CHUNKS):
                halo_copy(side, inner, g, h).wait_send()
    for i, h in plane:
        for stage in range(2):
            for g in range(CHUNKS):
                gather_copy(stage, g, i, h).wait_send()

    def landed(slot):
        copy_of(
            own_block, sums.at[slot], sum_send.at[slot], sum_recv.at[slot], (band, other, dy)
        ).wait_recv()

    @pl.when(dy == band)
    def _():
        result = own_block[...].astype(jnp.float32)
        for j in range(1, n_dy):
            slot = lax.rem(dy + j, n_dy) * n_band + band
            landed(slot)
            result = result + sums[slot].astype(jnp.float32)
        pair_out[...] = result

    @pl.when(dy != band)
    def _():
        own_copy(dy).wait_send()
        result = block[band, dy].astype(jnp.float32)
        for j in range(1, n_chips):
            slot = lax.rem(here + j, n_chips)
            landed(slot)
            result = result + sums[slot].astype(jnp.float32)
        pair_out[...] = result

    result = pair_out[...]
    copy = send(pair_out, pair_in, pair_send.at[0], pair_recv.at[0], (band, other, dy))
    copy.wait()
    each_target(lambda copy: copy.wait_send())

    result = (result + pair_in[...]) * (1.0 / cells_all)
    corr_ref[pl.ds(0, half), :] = result[:, :64]
    corr_ref[pl.ds(half, half), :] = pltpu.roll(result, 64, 1)[:, :64]


def store(filtered, correlation, filtered_hbm, correlation_hbm, sem):
    pairs = ((correlation, correlation_hbm), (filtered, filtered_hbm))
    copies = [pltpu.make_async_copy(a, b, sem.at[i]) for i, (a, b) in enumerate(pairs)]
    for copy in copies:
        copy.start()
    for copy in copies:
        copy.wait()


def fused(psi, base_potential, defect_site, defect_level):
    nb, nx, ny, nz = psi.shape
    n_band, n_dy = lax.axis_size("band"), lax.axis_size("dy")
    half, per = nb // 2, ny // n_band
    cells_all = nx * ny * nz * 2 * n_dy
    dma = pltpu.SemaphoreType.DMA
    n_plane, n_chips = 2 * n_band, n_band * n_dy
    vmem = pl.BlockSpec(memory_space=pltpu.VMEM)
    hbm = pl.BlockSpec(memory_space=pltpu.HBM)
    packed = (half, 128)
    filtered, correlation = pl.pallas_call(
        functools.partial(kernel, n_band, n_dy, cells_all),
        out_shape=(
            pltpu.VMEM(psi.shape, jnp.bfloat16),
            pltpu.VMEM((nb, nb * n_band // n_dy), jnp.float32),
        ),
        in_specs=[hbm, hbm, hbm, hbm],
        out_specs=(vmem, vmem),
        scratch_shapes=[
            pltpu.SMEM(defect_level.shape, jnp.float32),
            pltpu.VMEM(psi.shape, jnp.bfloat16),
            pltpu.VMEM(base_potential.shape, jnp.float32),
            pltpu.VMEM(defect_site.shape, jnp.int32),
            pltpu.VMEM(base_potential.shape, jnp.float32),
            pltpu.VMEM(base_potential.shape, jnp.float32),
            pltpu.VMEM((2, 4, nz), jnp.float32),
            pltpu.VMEM((2, 2, 4, nz), jnp.float32),
            pltpu.VMEM((nx, ny, nb, nz), jnp.bfloat16),
            pltpu.VMEM((2 * nx, ny + 4, 8, nz), jnp.float32),
            pltpu.VMEM((2 * nx, ny + 8, half, nz), jnp.bfloat16),
            pltpu.VMEM((2 * nx, ny + 8, half, nz), jnp.float32),
            pltpu.VMEM((2 * nx, ny + 4, half, nz), jnp.float32),
            pltpu.VMEM((2 * nx, ny, half, nz), jnp.bfloat16),
            pltpu.VMEM((nx, ny, nb, nz), jnp.bfloat16),
            pltpu.VMEM((nx, per, nb * n_band, nz), jnp.bfloat16),
            pltpu.VMEM((n_band, n_dy) + packed, jnp.bfloat16),
            pltpu.VMEM(packed, jnp.bfloat16),
            pltpu.VMEM((n_chips,) + packed, jnp.bfloat16),
            pltpu.VMEM(packed, jnp.float32),
            pltpu.VMEM(packed, jnp.float32),
            dma((2 * CHUNKS + 3,)), dma((CHUNKS,)), dma((CHUNKS,)), dma((4 * CHUNKS,)), dma((4 * CHUNKS,)),
            dma((1,)), dma((1,)), dma((4,)), dma((4,)),
            dma((2 * n_plane * CHUNKS,)), dma((2 * n_plane * CHUNKS,)),
            dma((2 * CHUNKS,)), dma((2 * CHUNKS,)),
            dma((n_chips,)), dma((n_chips,)), dma((1,)), dma((1,)),
            pltpu.SemaphoreType.REGULAR((2,)),
        ],
        compiler_params=pltpu.CompilerParams(
            collective_id=0, has_side_effects=True, vmem_limit_bytes=64 * 1024 * 1024 - 400 * 1024
        ),
    )(defect_level, psi, base_potential, defect_site)
    return pl.pallas_call(
        store,
        out_shape=(
            jax.ShapeDtypeStruct(filtered.shape, filtered.dtype),
            jax.ShapeDtypeStruct(correlation.shape, correlation.dtype),
        ),
        in_specs=[vmem, vmem],
        out_specs=(hbm, hbm),
        scratch_shapes=[dma((2,))],
    )(*(pltpu.with_memory_space_constraint(a, pltpu.VMEM) for a in (filtered, correlation)))


def solution(mesh):
    in_specs = (P("band", "dx", "dy", None), P("dx", "dy", None), P("dx", "dy", None), P())
    out_specs = (P("band", "dx", "dy", None), P("band", "dy"))
    n_band, n_dx, n_dy = mesh.shape["band"], mesh.shape["dx"], mesh.shape["dy"]

    def body(psi, base_potential, defect_site, defect_level):
        nb, nx, ny, nz = psi.shape
        fits = (
            n_dx == 2 and nx == 2 and nz == 128 and nb == 64
            and n_dy == 4 and n_band == 4 and ny == 8
        )
        run = fused if fits else shards
        return run(psi, base_potential, defect_site, defect_level)

    return jax.shard_map(body, mesh=mesh, in_specs=in_specs, out_specs=out_specs, check_vma=False)
```

```python
import functools

import jax
import jax.numpy as jnp
from jax import lax
from jax.experimental import pallas as pl
from jax.experimental.pallas import tpu as pltpu
from jax.sharding import PartitionSpec as P

SELF_WEIGHT = -2.5
NEAR_WEIGHT = 4.0 / 3.0
FAR_WEIGHT = -1.0 / 12.0
FILTER_CENTER = 5.5
FILTER_HALF = 3.5


def with_halo(block, sides, width):
    for axis, dim in sides:
        count = lax.axis_size(axis)
        forward = [(i, i + 1) for i in range(count - 1)]
        forward.append((count - 1, 0))
        backward = [(target, source) for source, target in forward]
        low = lax.ppermute(
            lax.slice_in_dim(block, block.shape[dim] - width, None, axis=dim), axis, forward
        )
        high = lax.ppermute(lax.slice_in_dim(block, 0, width, axis=dim), axis, backward)
        block = jnp.concatenate([low, block, high], axis=dim)
    return block


def hamiltonian(field, potential):
    padded = with_halo(field, (("dx", 1), ("dy", 2)), 2).astype(jnp.float32)
    width_x = field.shape[1]
    width_y = field.shape[2]
    center = padded[:, 2 : 2 + width_x, 2 : 2 + width_y, :]
    laplace = 3.0 * SELF_WEIGHT * center
    laplace = laplace + NEAR_WEIGHT * (
        padded[:, 3 : 3 + width_x, 2 : 2 + width_y, :]
        + padded[:, 1 : 1 + width_x, 2 : 2 + width_y, :]
    )
    laplace = laplace + FAR_WEIGHT * (
        padded[:, 4 : 4 + width_x, 2 : 2 + width_y, :] + padded[:, 0:width_x, 2 : 2 + width_y, :]
    )
    laplace = laplace + NEAR_WEIGHT * (
        padded[:, 2 : 2 + width_x, 3 : 3 + width_y, :]
        + padded[:, 2 : 2 + width_x, 1 : 1 + width_y, :]
    )
    laplace = laplace + FAR_WEIGHT * (
        padded[:, 2 : 2 + width_x, 4 : 4 + width_y, :] + padded[:, 2 : 2 + width_x, 0:width_y, :]
    )
    laplace = laplace + NEAR_WEIGHT * (jnp.roll(center, 1, 3) + jnp.roll(center, -1, 3))
    laplace = laplace + FAR_WEIGHT * (jnp.roll(center, 2, 3) + jnp.roll(center, -2, 3))
    return (-0.5 * laplace + potential[None] * center, center)


def shards(psi, base_potential, defect_site, defect_level):
    levels = jnp.arange(defect_level.shape[0], dtype=jnp.int32)
    picked = jnp.sum(
        jnp.where(
            defect_site[None] == levels[:, None, None, None],
            defect_level[:, None, None, None],
            jnp.float32(0.0),
        ),
        axis=0,
    )
    potential = base_potential + picked
    applied, start_field = hamiltonian(psi, potential)
    first = ((applied - FILTER_CENTER * start_field) / FILTER_HALF).astype(jnp.bfloat16)
    applied_next, first_wide = hamiltonian(first, potential)
    filtered = (
        2.0 * (applied_next - FILTER_CENTER * first_wide) / FILTER_HALF - start_field
    ).astype(jnp.bfloat16)
    nb_dev = psi.shape[0]
    cells_all = (
        psi.shape[1] * psi.shape[2] * psi.shape[3] * lax.axis_size("dx") * lax.axis_size("dy")
    )
    flat = filtered.reshape(nb_dev, -1)
    tile = lax.dot_general(
        flat,
        lax.all_gather(flat, "band", axis=0, tiled=True),
        (((1,), (1,)), ((), ())),
        preferred_element_type=jnp.float32,
    )
    column_part = lax.psum_scatter(
        tile.astype(jnp.bfloat16), "dy", scatter_dimension=1, tiled=True
    ).astype(jnp.float32)
    columns = lax.psum(column_part, "dx")
    correlation = columns / cells_all
    return (filtered, correlation)


MESH = pl.DeviceIdType.MESH
CHUNKS = 2


def apply_filter(load, x, j, coef):
    center = load(x, j)
    near = load((x + 1) % 4, j) + load((x + 3) % 4, j)
    far_x = load((x + 2) % 4, j)
    far = far_x + far_x
    near = near + load(x, j + 1) + load(x, j - 1)
    far = far + load(x, j + 2) + load(x, j - 2)
    near = near + pltpu.roll(center, 1, 1) + pltpu.roll(center, 127, 1)
    far = far + pltpu.roll(center, 2, 1) + pltpu.roll(center, 126, 1)
    rows = center.shape[0]
    scaled = (center.reshape(rows // 8, 8, 128) * coef[None]).reshape(rows, 128)
    return (
        scaled
        + near * (-0.5 * NEAR_WEIGHT / FILTER_HALF)
        + far * (-0.5 * FAR_WEIGHT / FILTER_HALF)
    )


def over(low, count, body, part):
    group = next(size for size in (8, 4, 2, 1) if count % size == 0)

    def step(i, carry):
        for k in range(group):
            body(part, low + i * group + k)
        return carry

    lax.fori_loop(0, count // group, step, 0)


def kernel(
    n_band, n_dy, cells_all,
    level_hbm, psi_hbm, base_hbm, site_hbm,
    out_ref, corr_ref,
    level_ref, psi_ref, base_ref, site_ref, weight, weight_in, edge, edge_in,
    psi_t, coef, halo, wide, first, done, out_t, gather, block, own_block, sums, pair_out, pair_in,
    load_sem, pair_psi_send, pair_psi_recv, psi_send, psi_recv, weight_send, weight_recv,
    edge_send, edge_recv, gather_send, gather_recv, out_send, out_recv, sum_send, sum_recv,
    pair_send, pair_recv, greeted,
):
    band, core, dy = lax.axis_index("band"), lax.axis_index("dx"), lax.axis_index("dy")
    nb = psi_ref.shape[0]
    half = nb // 2
    chunk = half // CHUNKS
    ny = psi_ref.shape[2]
    other = 1 - core
    side_a = (dy < n_dy // 2).astype(jnp.int32)
    side_b = 1 - side_a
    inner = dy + 2 * side_a - 1
    outer = lax.rem(dy - 2 * side_a + 1 + n_dy, n_dy)

    barrier = pltpu.get_barrier_semaphore()

    def signal(semaphore, device):
        pl.semaphore_signal(semaphore, inc=1, device_id=device, device_id_type=MESH)

    pieces = [pl.ds(h * half + g * chunk, chunk) for g in range(CHUNKS) for h in range(2)]
    loads = [
        pltpu.make_async_copy(src, dst, load_sem.at[index])
        for index, (src, dst) in enumerate(
            [(psi_hbm.at[rows], psi_ref.at[rows]) for rows in pieces]
            + [(level_hbm, level_ref), (site_hbm, site_ref), (base_hbm, base_ref)]
        )
    ]
    for load in loads:
        load.start()
    last = dy == n_dy - 1
    for h in range(2):
        signal(barrier, (band, h, inner))
    signal(barrier, (band, other, dy))

    @pl.when(jnp.logical_not(last))
    def _():
        for h in range(2):
            signal(barrier, (band, h, outer))

    @pl.when(dy < n_dy - 2)
    def _():
        for i in range(1, n_band):
            for h in range(2):
                signal(barrier, (lax.rem(band + i, n_band), h, dy))

    @pl.when(last)
    def _():
        pl.semaphore_wait(barrier, 5)
        signal(greeted.at[0], (band, core, 0))

    for load in loads[2 * CHUNKS :]:
        load.wait()

    site = site_ref[...]
    picked = jnp.zeros(site.shape, jnp.float32)
    for level in range(level_ref.shape[0]):
        picked = picked + jnp.where(site == level, level_ref[level], jnp.float32(0.0))
    weight[...] = (
        base_ref[...] + picked - (1.5 * SELF_WEIGHT + FILTER_CENTER)
    ) * (1.0 / FILTER_HALF)
    for x in range(2):
        edge[0, 2 * x : 2 * x + 2] = weight[x, ny - 2 : ny]
        edge[1, 2 * x : 2 * x + 2] = weight[x, 0:2]

    def turn(g):
        for h in range(2):
            loads[2 * g + h].wait()
            rows = pieces[2 * g + h]
            for x in range(2):
                psi_t[x, :, rows] = jnp.transpose(
                    psi_ref[rows, x].astype(jnp.float32), (1, 0, 2)
                ).astype(jnp.bfloat16)

    turn(0)

    @pl.when(dy == 0)
    def _():
        pl.semaphore_wait(barrier, 2 * n_band + 1)

    @pl.when(dy == 1)
    def _():
        pl.semaphore_wait(barrier, 2 * n_band + 3)

    @pl.when(dy == n_dy - 2)
    def _():
        pl.semaphore_wait(barrier, 5)


    layers = pl.ds(2 * core, 2)

    def copy_of(src, dst, send_sem, recv_sem, device):
        return pltpu.make_async_remote_copy(
            src_ref=src, dst_ref=dst, send_sem=send_sem, recv_sem=recv_sem,
            device_id=device, device_id_type=MESH,
        )

    def send(*args):
        copy = copy_of(*args)
        copy.start()
        return copy

    def bands(where, g):
        return pl.ds(pl.multiple_of(where * half + g * chunk, chunk), chunk)

    def part_of(g):
        return pl.ds(g * chunk, chunk)

    def halo_copy(side, target, g, h):
        slot = (side * CHUNKS + g) * 2
        return copy_of(
            psi_t.at[:, pl.ds((1 - side) * (ny - 4), 4), bands(h, g)],
            halo.at[layers, pl.ds(side * (ny + 4), 4), part_of(g)],
            psi_send.at[slot + h], psi_recv.at[slot + core], (band, h, target),
        )

    def edge_copy(side, target, h):
        return copy_of(
            edge.at[side], edge_in.at[side, core],
            edge_send.at[2 * side + h], edge_recv.at[2 * side + core], (band, h, target),
        )

    def send_part(g, side, target):
        for h in range(2):
            if g == 0:
                edge_copy(side, target, h).start()
            halo_copy(side, target, g, h).start()

    def send_side(side, target):
        for g in range(CHUNKS):
            send_part(g, side, target)

    @pl.when(dy > 0)
    def _():
        send_part(0, side_b, inner)
        send_part(0, side_a, outer)

    turn(1)

    @pl.when(dy > 0)
    def _():
        send_part(1, side_b, inner)
        send_part(1, side_a, outer)

    pairs = [
        send(
            psi_t.at[:, :, bands(other, g)], halo.at[layers, pl.ds(4, ny), part_of(g)],
            pair_psi_send.at[g], pair_psi_recv.at[g], (band, other, dy),
        )
        for g in range(CHUNKS)
    ]
    potential = send(
        weight, weight_in, weight_send.at[0], weight_recv.at[0], (band, other, dy)
    )

    @pl.when(dy == 0)
    def _():
        send_side(side_b, inner)
        pl.semaphore_wait(greeted.at[0], 1)
        send_side(side_a, outer)

    @pl.when(dy == n_dy - 2)
    def _():
        pl.semaphore_wait(greeted.at[1], 1)

    @pl.when(jnp.logical_and(dy > 0, jnp.logical_not(last)))
    def _():
        for i in range(1, n_band):
            signal(greeted.at[0], (lax.rem(band + i, n_band), core, dy))
        pl.semaphore_wait(greeted.at[0], n_band - 1)
        signal(greeted.at[1], (band, core, dy + 1))

    own = pl.ds(pl.multiple_of(core * half, half), half)
    for x in range(2):
        for y in range(ny):
            coef[2 * core + x, 2 + y] = jnp.broadcast_to(weight[x, y : y + 1], (8, 128))
            wide[2 * core + x, 4 + y] = psi_t[x, y, own].astype(jnp.float32)

    potential.wait()
    for x in range(2):
        for y in range(ny):
            coef[2 * other + x, 2 + y] = jnp.broadcast_to(weight_in[x, y : y + 1], (8, 128))

    def step_one(part, j):
        for x in range(4):
            value = apply_filter(lambda a, r: wide[a, r, part], x, j + 2, coef[x, j])
            first[x, j, part] = value.astype(jnp.bfloat16).astype(jnp.float32)

    def step_two(part, y):
        for x in range(4):
            value = apply_filter(lambda a, r: first[a, r, part], x, y + 2, coef[x, y + 2])
            done[x, y, part] = (2.0 * value - wide[x, y + 4, part]).astype(jnp.bfloat16)

    def widen(part, j):
        for x in range(4):
            wide[x, j, part] = halo[x, j, part].astype(jnp.float32)

    for g in range(CHUNKS):
        part = part_of(g)
        pairs[g].wait()
        for x in range(2):
            for y in range(ny):
                wide[2 * other + x, 4 + y, part] = halo[2 * other + x, 4 + y, part].astype(jnp.float32)
        over(4, ny - 4, step_one, part)

    me = 2 * band + core
    turned = (n_band - 1 - band, lax.rem(band + 2, n_band), band + 1 - 2 * lax.rem(band, 2), band)
    plane = [(i, lax.rem(core + h, 2)) for i in turned[:-1] for h in range(2)] + [(band, other)]
    def row_of(side, i):
        return side * (ny // 2) + i

    def out_copy(stage, g):
        rows = pl.ds(sides[stage] * (ny // 2), ny // 2)
        place = pl.ds(pl.multiple_of(core * half + g * chunk, chunk), chunk)
        return copy_of(
            done.at[pl.ds(2 * other, 2), rows, part_of(g)], out_t.at[:, rows, place],
            out_send.at[stage * CHUNKS + g], out_recv.at[stage * CHUNKS + g], (band, other, dy),
        )

    def gather_copy(stage, g, i, h):
        place = pl.ds(pl.multiple_of(band * nb + core * half + g * chunk, chunk), chunk)
        slot = stage * CHUNKS + g
        return copy_of(
            done.at[pl.ds(2 * h, 2), row_of(sides[stage], i), part_of(g)],
            gather.at[:, stage, place],
            gather_send.at[(i * 2 + h) * 2 * CHUNKS + slot], gather_recv.at[me * 2 * CHUNKS + slot],
            (i, h, dy),
        )

    sides = (side_a, side_b)

    @pl.when(last)
    def _():
        pl.semaphore_wait(greeted.at[1], 1)

    for stage, side in enumerate(sides):
        for g in range(CHUNKS):
            part = part_of(g)
            if g == 0:
                for h in range(2):
                    copy_of(
                        edge.at[side], edge_in.at[side, h],
                        edge_send.at[2 * side + h], edge_recv.at[2 * side + h], (band, h, inner),
                    ).wait_recv()
                for source in range(2):
                    for x in range(2):
                        for y in range(2):
                            coef[2 * source + x, side * (ny + 2) + y] = jnp.broadcast_to(
                                edge_in[side, source, 2 * x + y : 2 * x + y + 1], (8, 128)
                            )
            for h in range(2):
                slot = (side * CHUNKS + g) * 2 + h
                copy_of(
                    psi_t.at[:, pl.ds(0, 4), bands(h, g)],
                    halo.at[pl.ds(2 * h, 2), pl.ds(side * (ny + 4), 4), part],
                    psi_send.at[slot], psi_recv.at[slot], (band, h, inner),
                ).wait_recv()
            over(side * (ny + 4), 4, widen, part)
            over(side * ny, 4, step_one, part)
            over(side * (ny // 2), ny // 2, step_two, part)
            for i, h in plane:
                gather_copy(stage, g, i, h).start()

            out_copy(stage, g).start()

    for g in range(CHUNKS):
        place = pl.ds(pl.multiple_of(band * nb + core * half + g * chunk, chunk), chunk)
        for x in range(2):
            for stage in range(2):
                gather[x, stage, place] = done[2 * core + x, row_of(sides[stage], band), part_of(g)]
    for x in range(2):
        for y in range(ny):
            out_t[x, y, own] = done[2 * core + x, y]
    for stage in range(2):
        for g in range(CHUNKS):
            out_copy(stage, g).wait()

    def pack(tile):
        top, bottom = tile[:half], tile[half:]
        return (
            jnp.where(low, top, pltpu.roll(bottom, 64, 1)).astype(jnp.bfloat16),
            jnp.where(low, pltpu.roll(top, 64, 1), bottom).astype(jnp.bfloat16),
        )

    low = lax.broadcasted_iota(jnp.int32, (half, 128), 1) < 64
    cells = jnp.concatenate([out_t[x, y] for x in range(2) for y in range(ny)], axis=1)
    square = lax.dot_general(
        cells, cells, (((1,), (1,)), ((), ())), preferred_element_type=jnp.float32
    )
    square = jnp.concatenate([square, square], axis=1)
    own_block[...] = jnp.where(low, square[:half], square[half:]).astype(jnp.bfloat16)

    def own_copy(slot):
        return copy_of(
            own_block, sums.at[slot * n_band + band],
            sum_send.at[band * n_band + band], sum_recv.at[slot * n_band + band],
            (band, core, band),
        )

    @pl.when(dy != band)
    def _():
        own_copy(dy).start()

    for j in range(1, 2 * n_band):
        source = lax.rem(me + j, 2 * n_band)
        for g in range(CHUNKS):
            place = pl.ds(pl.multiple_of(source * half + g * chunk, chunk), chunk)
            for stage in range(2):
                slot = source * 2 * CHUNKS + stage * CHUNKS + g
                copy_of(
                    gather.at[:, stage, place], gather.at[:, stage, place],
                    gather_send.at[slot], gather_recv.at[slot],
                    (lax.div(source, 2), lax.rem(source, 2), dy),
                ).wait_recv()

    total = None
    for x in range(2):
        cells = jnp.concatenate([gather[x, y] for y in range(2)], axis=1)
        term = lax.dot_general(
            cells, cells, (((1,), (1,)), ((), ())), preferred_element_type=jnp.float32
        )
        total = term if total is None else total + term
    for i in range(n_band):
        for k in range(n_dy // 2):
            tile = total[nb * i : nb * i + nb, 128 * k : 128 * k + 128]
            block[i, 2 * k], block[i, 2 * k + 1] = pack(tile)
    here = dy * n_band + band
    n_chips = n_band * n_dy

    def sum_copy(to_band, to_dy):
        return copy_of(
            block.at[to_band, to_dy], sums.at[here], sum_send.at[to_dy * n_band + to_band],
            sum_recv.at[here], (to_band, core, to_dy),
        )

    low_half = (dy < n_dy // 2).astype(jnp.int32)
    targets = [
        (i, low_half * (n_dy - 1 - k) + (1 - low_half) * k) for k in range(n_dy) for i in turned
    ]

    def each_target(act):
        for to_band, to_dy in targets:
            itself = jnp.logical_and(to_band == band, to_dy == dy)

            @pl.when(jnp.logical_not(jnp.logical_or(itself, to_dy == to_band)))
            def _():
                act(sum_copy(to_band, to_dy))

    each_target(lambda copy: copy.start())

    for x in range(2):
        out_ref[:, x] = jnp.transpose(out_t[x].astype(jnp.float32), (1, 0, 2)).astype(jnp.bfloat16)
    for side in range(2):
        for h in range(2):
            edge_copy(side, inner, h).wait_send()
            for g in range(CHUNKS):
                halo_copy(side, inner, g, h).wait_send()
    for i, h in plane:
        for stage in range(2):
            for g in range(CHUNKS):
                gather_copy(stage, g, i, h).wait_send()

    def landed(slot):
        copy_of(
            own_block, sums.at[slot], sum_send.at[slot], sum_recv.at[slot], (band, other, dy)
        ).wait_recv()

    @pl.when(dy == band)
    def _():
        result = own_block[...].astype(jnp.float32)
        for j in range(1, n_dy):
            slot = lax.rem(dy + j, n_dy) * n_band + band
            landed(slot)
            result = result + sums[slot].astype(jnp.float32)
        pair_out[...] = result

    @pl.when(dy != band)
    def _():
        own_copy(dy).wait_send()
        result = block[band, dy].astype(jnp.float32)
        for j in range(1, n_chips):
            slot = lax.rem(here + j, n_chips)
            landed(slot)
            result = result + sums[slot].astype(jnp.float32)
        pair_out[...] = result

    result = pair_out[...]
    copy = send(pair_out, pair_in, pair_send.at[0], pair_recv.at[0], (band, other, dy))
    each_target(lambda copy: copy.wait_send())
    copy.wait()

    result = (result + pair_in[...]) * (1.0 / cells_all)
    corr_ref[pl.ds(0, half), :] = result[:, :64]
    corr_ref[pl.ds(half, half), :] = pltpu.roll(result, 64, 1)[:, :64]


def store(filtered, correlation, filtered_hbm, correlation_hbm, sem):
    pairs = ((correlation, correlation_hbm), (filtered, filtered_hbm))
    copies = [pltpu.make_async_copy(a, b, sem.at[i]) for i, (a, b) in enumerate(pairs)]
    for copy in copies:
        copy.start()
    for copy in copies:
        copy.wait()


def fused(psi, base_potential, defect_site, defect_level):
    nb, nx, ny, nz = psi.shape
    n_band, n_dy = lax.axis_size("band"), lax.axis_size("dy")
    half, per = nb // 2, ny // n_band
    cells_all = nx * ny * nz * 2 * n_dy
    dma = pltpu.SemaphoreType.DMA
    n_plane, n_chips = 2 * n_band, n_band * n_dy
    vmem = pl.BlockSpec(memory_space=pltpu.VMEM)
    hbm = pl.BlockSpec(memory_space=pltpu.HBM)
    packed = (half, 128)
    filtered, correlation = pl.pallas_call(
        functools.partial(kernel, n_band, n_dy, cells_all),
        out_shape=(
            pltpu.VMEM(psi.shape, jnp.bfloat16),
            pltpu.VMEM((nb, nb * n_band // n_dy), jnp.float32),
        ),
        in_specs=[hbm, hbm, hbm, hbm],
        out_specs=(vmem, vmem),
        scratch_shapes=[
            pltpu.SMEM(defect_level.shape, jnp.float32),
            pltpu.VMEM(psi.shape, jnp.bfloat16),
            pltpu.VMEM(base_potential.shape, jnp.float32),
            pltpu.VMEM(defect_site.shape, jnp.int32),
            pltpu.VMEM(base_potential.shape, jnp.float32),
            pltpu.VMEM(base_potential.shape, jnp.float32),
            pltpu.VMEM((2, 4, nz), jnp.float32),
            pltpu.VMEM((2, 2, 4, nz), jnp.float32),
            pltpu.VMEM((nx, ny, nb, nz), jnp.bfloat16),
            pltpu.VMEM((2 * nx, ny + 4, 8, nz), jnp.float32),
            pltpu.VMEM((2 * nx, ny + 8, half, nz), jnp.bfloat16),
            pltpu.VMEM((2 * nx, ny + 8, half, nz), jnp.float32),
            pltpu.VMEM((2 * nx, ny + 4, half, nz), jnp.float32),
            pltpu.VMEM((2 * nx, ny, half, nz), jnp.bfloat16),
            pltpu.VMEM((nx, ny, nb, nz), jnp.bfloat16),
            pltpu.VMEM((nx, per, nb * n_band, nz), jnp.bfloat16),
            pltpu.VMEM((n_band, n_dy) + packed, jnp.bfloat16),
            pltpu.VMEM(packed, jnp.bfloat16),
            pltpu.VMEM((n_chips,) + packed, jnp.bfloat16),
            pltpu.VMEM(packed, jnp.float32),
            pltpu.VMEM(packed, jnp.float32),
            dma((2 * CHUNKS + 3,)), dma((CHUNKS,)), dma((CHUNKS,)), dma((4 * CHUNKS,)), dma((4 * CHUNKS,)),
            dma((1,)), dma((1,)), dma((4,)), dma((4,)),
            dma((2 * n_plane * CHUNKS,)), dma((2 * n_plane * CHUNKS,)),
            dma((2 * CHUNKS,)), dma((2 * CHUNKS,)),
            dma((n_chips,)), dma((n_chips,)), dma((1,)), dma((1,)),
            pltpu.SemaphoreType.REGULAR((2,)),
        ],
        compiler_params=pltpu.CompilerParams(
            collective_id=0, has_side_effects=True, vmem_limit_bytes=64 * 1024 * 1024 - 400 * 1024
        ),
    )(defect_level, psi, base_potential, defect_site)
    return pl.pallas_call(
        store,
        out_shape=(
            jax.ShapeDtypeStruct(filtered.shape, filtered.dtype),
            jax.ShapeDtypeStruct(correlation.shape, correlation.dtype),
        ),
        in_specs=[vmem, vmem],
        out_specs=(hbm, hbm),
        scratch_shapes=[dma((2,))],
    )(*(pltpu.with_memory_space_constraint(a, pltpu.VMEM) for a in (filtered, correlation)))


def solution(mesh):
    in_specs = (P("band", "dx", "dy", None), P("dx", "dy", None), P("dx", "dy", None), P())
    out_specs = (P("band", "dx", "dy", None), P("band", "dy"))
    n_band, n_dx, n_dy = mesh.shape["band"], mesh.shape["dx"], mesh.shape["dy"]

    def body(psi, base_potential, defect_site, defect_level):
        nb, nx, ny, nz = psi.shape
        fits = (
            n_dx == 2 and nx == 2 and nz == 128 and nb == 64
            and n_dy == 4 and n_band == 4 and ny == 8
        )
        run = fused if fits else shards
        return run(psi, base_potential, defect_site, defect_level)

    return jax.shard_map(body, mesh=mesh, in_specs=in_specs, out_specs=out_specs, check_vma=False)
```
